32 devices in a mesh: lat: 8 (over z, y), lon: 4 (over x, core).
Axes of the slice: x: 2, y: 2, z: 4, core: 2. Of those that a mesh axis runs over, the one named last changes fastest.
Arguments:
- state_fields: float32 [5, 32, 64, 4096], P(None, None, 'lat', 'lon'), may hold values from -6 to 6
- stencil_weights: float32 [4, 32, 64, 4096], P(None, None, 'lat', 'lon'), may hold values from 0.02 to 0.22
- filter_mask: int32 [64], replicated, may hold values from 0 to 1, as said below
- cutoff_wave: int32 [64], replicated, may hold values from 0 to 255, as said below
Outputs:
- advanced: float32 [5, 32, 64, 4096], P(None, None, 'lat', 'lon')
The draws below stay inside these ranges and needn't reach their ends.
Inputs may be any that keep to these rules, and one draw needn't show every extreme that they name: `filter_mask`: every row outside the first and last 8 rows holds 0. `cutoff_wave`: from 1 to 255 in the first and last 8 rows, 0 elsewhere.
All inputs are finite; a program needn't handle non-finite values.
Results may differ from the reference program's by a relative error of at most 0.0011.
Values may be sent and summed in bfloat16 or wider, within the bound.
A program may use at most 64 MiB of HBM per device.

```python
import math
import jax
import jax.numpy as jnp
from jax import lax

NLON = 4096
FIELDS = 5
LEV = 32
KC = 256
NLAT = 64
POLAR = 8


def polar_row(choice_value):
    return jnp.where(choice_value < POLAR, choice_value, NLAT - 2 * POLAR + choice_value)


def draw_filter_mask(key, part):
    row_ids = jnp.arange(NLAT, dtype=jnp.int32)
    inside = (row_ids < POLAR) | (row_ids >= NLAT - POLAR)
    coins = jax.random.randint(jax.random.fold_in(key, 11), (NLAT,), 0, 4)
    picked = polar_row(jax.random.randint(jax.random.fold_in(key, 12), (), 0, 2 * POLAR))
    chosen = inside & ((coins != 0) | (row_ids == picked))
    return jnp.where(chosen, 1, 0).astype(jnp.int32)


def draw_cutoff_wave(key, part):
    row_ids = jnp.arange(NLAT, dtype=jnp.int32)
    inside = (row_ids < POLAR) | (row_ids >= NLAT - POLAR)
    values = jax.random.randint(jax.random.fold_in(key, 21), (NLAT,), 1, KC)
    lowest = polar_row(jax.random.randint(jax.random.fold_in(key, 22), (), 0, 2 * POLAR))
    highest = polar_row(jax.random.randint(jax.random.fold_in(key, 23), (), 0, 2 * POLAR))
    values = jnp.where(row_ids == lowest, 1, values)
    values = jnp.where(row_ids == highest, KC - 1, values)
    return jnp.where(inside, values, 0).astype(jnp.int32)


def shard_levels(stream_key, extent, split, smallest, high):
    factor_of, own = 1.0, jax.random.fold_in(stream_key, 6)
    for position, shards_of in split:
        heights = jnp.exp(jax.random.uniform(jax.random.fold_in(own, position), (shards_of,), jnp.float32, smallest / len(split), high / len(split)))
        factor_of = factor_of * jnp.repeat(heights, extent[position] // shards_of).reshape([-1 if axis == position else 1 for axis in range(len(extent))])
    return factor_of


def normal_values(rng, extent, deviation, bound, pieces=(), kind=jnp.bfloat16):
    result = jax.random.normal(rng, extent, jnp.float32) * deviation
    if len(pieces) > 0:
        result = shard_levels(rng, extent, pieces, -0.22, 0.18) * result
    return jnp.clip(result, min=-bound, max=bound).astype(kind)


def setup_inputs(seed: int = 0) -> dict:
    streams_of = jax.random.split(jax.random.key(seed), 5)
    state_fields = normal_values(streams_of[0], (FIELDS, LEV, NLAT, NLON), 1.0, 6.0, ((2, 8), (3, 4)), jnp.float32)
    stencil_weights = jnp.clip(0.02 + 0.2 * jax.random.uniform(streams_of[1], (4, LEV, NLAT, NLON), jnp.float32) ** shard_levels(streams_of[1], (4, LEV, NLAT, NLON), ((2, 8), (3, 4)), -0.2, 0.2), 0.02, 0.22)
    filter_mask = draw_filter_mask(jax.random.fold_in(streams_of[4], 71), 0)
    cutoff_wave = draw_cutoff_wave(jax.random.fold_in(streams_of[4], 71), 0)
    return {"state_fields": state_fields, "stencil_weights": stencil_weights, "filter_mask": filter_mask, "cutoff_wave": cutoff_wave}


def wave_table(columns, mode_count, circle_size):
    wavenums = jnp.arange(2 * mode_count, dtype=jnp.int32) % mode_count
    product = (columns[:, None] * wavenums[None, :]) % circle_size
    angles = product.astype(jnp.float32) * (2.0 * math.pi / circle_size)
    upper = jnp.arange(2 * mode_count, dtype=jnp.int32) < mode_count
    return jnp.where(upper[None, :], jnp.cos(angles), jnp.sin(angles)).astype(jnp.bfloat16)


def mode_scale(cutoffs, mode_count, circle_size):
    wavenums = jnp.arange(2 * mode_count, dtype=jnp.int32) % mode_count
    weights = jnp.where(wavenums == 0, 1.0 / circle_size, 2.0 / circle_size).astype(jnp.float32)
    return jnp.where(wavenums[None, :] <= cutoffs[:, None], weights[None, :], jnp.float32(0.0)).astype(jnp.float32)


def reference(state_fields, stencil_weights, filter_mask, cutoff_wave):
    field = state_fields
    wind_signs = jnp.where(jnp.arange(FIELDS) < 2, -1.0, 1.0).astype(jnp.float32)[:, None, None, None]
    turned = jnp.roll(field, NLON // 2, axis=3)
    north_side = jnp.concatenate([wind_signs * turned[:, :, 0:1], field[:, :, :-1]], axis=2)
    south_side = jnp.concatenate([field[:, :, 1:], wind_signs * turned[:, :, -1:]], axis=2)
    east_side = jnp.roll(field, -1, axis=3)
    west_side = jnp.roll(field, 1, axis=3)
    weights = stencil_weights
    stepped = field + weights[0] * (east_side - field) + weights[1] * (west_side - field) + weights[2] * (north_side - field) + weights[3] * (south_side - field)
    band_index = jnp.concatenate([jnp.arange(POLAR, dtype=jnp.int32), jnp.arange(NLAT - POLAR, NLAT, dtype=jnp.int32)]).astype(jnp.int32)
    band_values = stepped[:, :, band_index, :]
    rounded = lax.optimization_barrier(band_values.astype(jnp.bfloat16)).astype(jnp.float32)
    circle_table = lax.optimization_barrier(wave_table(jnp.arange(NLON, dtype=jnp.int32), KC, NLON)).astype(jnp.float32)
    spectra = jnp.dot(rounded.reshape(-1, NLON), circle_table, precision=lax.Precision.HIGHEST)
    spectra = spectra.reshape(FIELDS * LEV, 2 * POLAR, 2 * KC) * mode_scale(cutoff_wave[band_index], KC, NLON)[None]
    spectra = lax.optimization_barrier(spectra.astype(jnp.bfloat16)).astype(jnp.float32)
    smooth = jnp.dot(spectra.reshape(-1, 2 * KC), circle_table.T, precision=lax.Precision.HIGHEST)
    smooth = lax.optimization_barrier(smooth.astype(jnp.bfloat16)).astype(jnp.float32)
    smooth = smooth.reshape(FIELDS, LEV, 2 * POLAR, NLON)
    keep_rows = filter_mask[band_index] == 1
    chosen = jnp.where(keep_rows[None, None, :, None], smooth, band_values)
    return stepped.at[:, :, band_index, :].set(chosen)
```

```python
import math

import jax
import jax.numpy as jnp
import numpy as np
from jax import lax
from jax.experimental import pallas as pl
from jax.experimental.pallas import tpu as pltpu
from jax.sharding import PartitionSpec as P

KC = 256


def angle_parts(columns, circle_size, axis):
    waves = lax.broadcasted_iota(
        jnp.int32, (columns.size, KC) if axis == 1 else (KC, columns.size), axis
    )
    product = jnp.expand_dims(columns, axis) * waves % circle_size
    angles = product.astype(jnp.float32) * (2.0 * math.pi / circle_size)
    return jnp.cos(angles), jnp.sin(angles)


MESH = pl.DeviceIdType.MESH


def step_kernel(
    state,
    weights,
    cosines,
    sines,
    turned_cosines,
    turned_sines,
    bounds,
    results,
    waves,
    turned,
    rounded,
    top,
    bottom,
    north,
    south,
    columns_out,
    columns_in,
    sides,
    partial,
    halves,
    quarters,
    half_in,
    quarter_in,
    spectra,
    row_send,
    row_recv,
    side_send,
    side_recv,
    sum_send,
    sum_recv,
    join_send,
    join_recv,
):
    fields, lines, columns = state.shape
    chunks, _, size, _ = top.shape
    depth = lines // chunks
    rows = depth // size
    modes = waves.shape[1] // 2
    half = partial.shape[1] // 2
    quarter = half // 2
    lat_count, lon_count = lax.axis_size("lat"), lax.axis_size("lon")
    lat, lon = lax.axis_index("lat"), lax.axis_index("lon")
    after = lax.rem(lon + 1, lon_count)
    before = lax.rem(lon + lon_count - 1, lon_count)
    across = lax.rem(lon + lon_count // 2, lon_count)
    bits = lon_count.bit_length() - 1
    digit = [lax.rem(lon // (1 << b), 2) for b in range(bits)]
    peer = [lon + (1 << b) - (2 << b) * digit[b] for b in range(bits)]
    own_half = digit[0] * half
    own_quarter = digit[1] * quarter

    def span_of(g, first, count):
        return pl.ds(pl.multiple_of(g * depth + first, count), count)

    def remote(source, target, sent, got, device):
        return pltpu.make_async_remote_copy(
            src_ref=source,
            dst_ref=target,
            send_sem=sent,
            recv_sem=got,
            device_id=device,
            device_id_type=MESH,
        )

    def row_copy(g, up, device, into_north):
        return remote(
            top.at[g] if up else bottom.at[g],
            north.at[g] if into_north else south.at[g],
            row_send.at[0 if up else 1, g],
            row_recv.at[0 if into_north else 1, g],
            device,
        )

    def side_copy(k, device):
        return remote(
            columns_out.at[k], columns_in.at[k], side_send.at[k], side_recv.at[k], device
        )

    def sum_copy(b, g):
        if b == 0:
            away = pl.ds(pl.multiple_of((1 - digit[0]) * half, 16), half)
            source, target = partial.at[g, away], half_in.at[g]
        elif b == 1:
            away = pl.ds(pl.multiple_of((1 - digit[1]) * quarter, 16), quarter)
            source, target = halves.at[g, away], quarter_in.at[0, g]
        else:
            source, target = quarters.at[b - 2, g], quarter_in.at[b - 1, g]
        return remote(source, target, sum_send.at[b, g], sum_recv.at[b, g], (lat, peer[b]))

    def join_copy(b, g):
        if b == 0:
            part = pl.ds(pl.multiple_of(own_half, 16), half)
        else:
            part = pl.ds(pl.multiple_of(own_half + own_quarter, 16), quarter)
        view = spectra.at[g, part]
        return remote(view, view, join_send.at[b, g], join_recv.at[b, g], (lat, peer[b]))

    barrier = pltpu.get_barrier_semaphore()
    for other in (after, before, across, *peer):
        pl.semaphore_signal(barrier, inc=1, device_id=(lat, other), device_id_type=MESH)

    @pl.when(lat > 0)
    def _():
        pl.semaphore_signal(barrier, inc=1, device_id=(lat - 1, lon), device_id_type=MESH)

    @pl.when(lat < lat_count - 1)
    def _():
        pl.semaphore_signal(barrier, inc=1, device_id=(lat + 1, lon), device_id_type=MESH)

    inside = (lat > 0) & (lat < lat_count - 1)

    @pl.when(inside)
    def _():
        pl.semaphore_wait(barrier, 5 + bits)

    @pl.when(jnp.logical_not(inside))
    def _():
        pl.semaphore_wait(barrier, 4 + bits)

    taker = lax.broadcasted_iota(jnp.int32, (2 * size, depth), 0)
    taken = lax.broadcasted_iota(jnp.int32, (2 * size, depth), 1)
    wanted = jnp.where(taker < size, taker * rows, (taker - size) * rows + rows - 1)
    gather = jnp.where(taken == wanted, 1.0, 0.0).astype(jnp.bfloat16)

    def send_rows(g, carry):
        for field in range(fields):
            sign = -1.0 if field < 2 else 1.0
            up_sign = jnp.where(lat == 0, sign, 1.0).astype(jnp.float32)
            down_sign = jnp.where(lat == lat_count - 1, sign, 1.0).astype(jnp.float32)
            edges = jnp.dot(
                gather,
                state[field, span_of(g, 0, depth)].astype(jnp.bfloat16),
                preferred_element_type=jnp.float32,
            )
            top[g, field] = (edges[:size] * up_sign).astype(jnp.bfloat16)
            bottom[g, field] = (edges[size:] * down_sign).astype(jnp.bfloat16)

        @pl.when(lat == 0)
        def _():
            row_copy(g, True, (lat, across), True).start()

        @pl.when(lat > 0)
        def _():
            row_copy(g, True, (lat - 1, lon), False).start()

        @pl.when(lat < lat_count - 1)
        def _():
            row_copy(g, False, (lat + 1, lon), True).start()

        @pl.when(lat == lat_count - 1)
        def _():
            row_copy(g, False, (lat, across), False).start()

        return carry

    lax.fori_loop(0, chunks, send_rows, 0)

    spot = lax.broadcasted_iota(jnp.int32, (16, 128), 1)
    line = lax.broadcasted_iota(jnp.int32, (16, 128), 0)

    def pick(k, lanes, lane):
        chosen = jnp.where((spot == lane) & (line == 0), 1.0, 0.0).astype(jnp.bfloat16)
        for g in range(chunks):
            for field in range(0, fields):
                first = (g * fields + field) * depth
                edge = state[field, span_of(g, 0, depth), lanes].astype(jnp.bfloat16)
                picked = lax.dot_general(
                    chosen, edge, (((1,), (1,)), ((), ())), preferred_element_type=jnp.float32
                )
                columns_out[k, g * fields + field] = picked.astype(jnp.bfloat16)

    pick(0, pl.ds(columns - 128, 128), 127)
    side_copy(0, (lat, after)).start()
    pick(1, pl.ds(0, 128), 0)
    side_copy(1, (lat, before)).start()

    fine = 32
    coarse = columns // fine
    fine_cos, fine_sin = cosines[coarse:], sines[coarse:]

    def fill(at, carry):
        span = pl.ds(pl.multiple_of(at * fine, fine), fine)
        coarse_cos, coarse_sin = cosines[pl.ds(at, 1)], sines[pl.ds(at, 1)]
        waves[span, :modes] = (coarse_cos * fine_cos - coarse_sin * fine_sin).astype(jnp.bfloat16)
        waves[span, modes:] = (coarse_sin * fine_cos + coarse_cos * fine_sin).astype(jnp.bfloat16)
        return carry

    lax.fori_loop(0, coarse, fill, 0)
    lane_cos, lane_sin = turned_cosines[:, :128], turned_sines[:, :128]
    for at in range(columns // 128):
        span = pl.ds(at * 128, 128)
        tile_cos = turned_cosines[:, 128 + at : 129 + at]
        tile_sin = turned_sines[:, 128 + at : 129 + at]
        turned[:modes, span] = (tile_cos * lane_cos - tile_sin * lane_sin).astype(jnp.bfloat16)
        turned[modes:, span] = (tile_sin * lane_cos + tile_cos * lane_sin).astype(jnp.bfloat16)

    spread = jnp.where(line == 0, 1.0, 0.0).astype(jnp.bfloat16)
    for k in range(2):
        side_copy(k, (lat, after)).wait_recv()
        for at in range(chunks * fields):
            sides[k, at] = lax.dot_general(
                columns_in[k, at],
                spread,
                (((0,), (0,)), ((), ())),
                preferred_element_type=jnp.float32,
            )

    lane = lax.broadcasted_iota(jnp.int32, (rows, columns), 1)
    level_line = lax.broadcasted_iota(jnp.int32, (rows, columns), 0)
    copies = columns // 128

    wave = lax.rem(lax.broadcasted_iota(jnp.int32, (rows, 2 * modes), 1), modes)
    circle_size = columns * lon_count
    weight = jnp.where(wave == 0, 1.0 / circle_size, 2.0 / circle_size)
    scale = jnp.where(wave <= bounds[:, 1:2], weight, 0.0).astype(jnp.float32)

    def advance(g):
        row_copy(g, True, (lat, across), True).wait_recv()
        row_copy(g, False, (lat, across), False).wait_recv()

        def one_field(field, inner):
            above = north[g, field].astype(jnp.float32)
            below = south[g, field].astype(jnp.float32)
            for level in range(0, size, 2):
                pair = []
                for at in (level, level + 1):
                    span = pl.ds(at * rows, rows)
                    here = span_of(g, at * rows, rows)
                    x = state[field, here]
                    left = jnp.concatenate([sides[0, g * fields + field, span]] * copies, axis=1)
                    right = jnp.concatenate([sides[1, g * fields + field, span]] * copies, axis=1)
                    w = jnp.where(lane == 0, left, pltpu.roll(x, 1, 1))
                    e = jnp.where(lane == columns - 1, right, pltpu.roll(x, columns - 1, 1))
                    n = jnp.where(level_line == 0, above[at : at + 1], pltpu.roll(x, 1, 0))
                    s = jnp.where(
                        level_line == rows - 1, below[at : at + 1], pltpu.roll(x, rows - 1, 0)
                    )
                    y = (
                        x
                        + weights[0, here] * (e - x)
                        + weights[1, here] * (w - x)
                        + weights[2, here] * (n - x)
                        + weights[3, here] * (s - x)
                    )
                    results[field, here] = y
                    pair.append(y)
                first = pl.multiple_of(field * depth + level * rows, 2 * rows)
                rounded[pl.ds(first, 2 * rows), :] = jnp.concatenate(pair, axis=0).astype(
                    jnp.bfloat16
                )
            return inner

        lax.fori_loop(0, fields, one_field, 0)
        partial[g] = jnp.dot(rounded[...], waves[...], preferred_element_type=jnp.float32)
        sum_copy(0, g).start()

    def pair_sum(g):
        sum_copy(0, g).wait_recv()
        mine = pl.ds(pl.multiple_of(own_half, 16), half)
        halves[g] = partial[g, mine] + half_in[g]
        sum_copy(1, g).start()

    def full_sum(g):
        sum_copy(1, g).wait_recv()
        mine = pl.ds(pl.multiple_of(own_quarter, 16), quarter)
        total = halves[g, mine] + quarter_in[0, g]
        for b in range(2, bits):
            quarters[b - 2, g] = total
            sum_copy(b, g).start()
            sum_copy(b, g).wait_recv()
            total = total + quarter_in[b - 1, g]
        scaled = total.reshape(quarter // rows, rows, 2 * modes) * scale[None]
        part = pl.ds(pl.multiple_of(own_half + own_quarter, 16), quarter)
        spectra[g, part] = scaled.reshape(quarter, 2 * modes).astype(jnp.bfloat16)
        join_copy(1, g).start()

    def join(g):
        join_copy(1, g).wait_recv()
        join_copy(0, g).start()

    def merge(g):
        join_copy(0, g).wait_recv()
        smooth = jnp.dot(spectra[g], turned[...], preferred_element_type=jnp.float32)
        smooth = smooth.astype(jnp.bfloat16).astype(jnp.float32)
        smooth = smooth.reshape(fields, size, rows, columns)
        kept = jnp.broadcast_to(bounds[:, 0:1], (rows, columns)) != 0
        for field in range(fields):
            for at in range(size):
                here = span_of(g, at * rows, rows)
                results[field, here] = jnp.where(kept, smooth[field, at], results[field, here])

    def forward(t, carry):
        advance(t)

        @pl.when(t >= 1)
        def _():
            pair_sum(t - 1)

        return carry

    last = chunks - 1
    lax.fori_loop(0, chunks, forward, 0)
    full_sum(0)
    pair_sum(last)

    def sums(g, carry):
        full_sum(g)
        return carry

    def joins(g, carry):
        join(g)
        return carry

    def merges(g, carry):
        merge(g)

        @pl.when(g + 2 < chunks)
        def _():
            join(g + 2)

        return carry

    lax.fori_loop(1, last, sums, 0)
    lax.fori_loop(0, 2, joins, 0)
    full_sum(last)
    lax.fori_loop(0, chunks, merges, 0)

    def finish(g, carry):
        for b in range(bits):
            sum_copy(b, g).wait_send()
        for b in range(2):
            join_copy(b, g).wait_send()
        row_copy(g, True, (lat, across), True).wait_send()
        row_copy(g, False, (lat, across), False).wait_send()
        return carry

    lax.fori_loop(0, chunks, finish, 0)
    for k in range(2):
        side_copy(k, (lat, after)).wait_send()


def on_device(state_fields, stencil_weights, filter_mask, cutoff_wave):
    fields, levels, rows, columns = state_fields.shape
    lat_count, lon_count = lax.axis_size("lat"), lax.axis_size("lon")
    lat_pos, lon_pos = lax.axis_index("lat"), lax.axis_index("lon")
    circle_size = columns * lon_count
    size = 8
    steps = levels // size
    start = lat_pos * rows
    bounds = lax.dynamic_slice_in_dim(jnp.stack([filter_mask, cutoff_wave], axis=1), start, rows)
    origin = lon_pos * columns
    cosines, sines = angle_parts(
        jnp.concatenate(
            [origin + 32 * jnp.arange(columns // 32), jnp.arange(32)]
        ).astype(jnp.int32),
        circle_size,
        1,
    )
    turned_cosines, turned_sines = angle_parts(
        jnp.concatenate(
            [jnp.arange(128), origin + 128 * jnp.arange(columns // 128)]
        ).astype(jnp.int32),
        circle_size,
        0,
    )
    rows_each = fields * size * rows
    depth = size * rows
    dma = pltpu.SemaphoreType.DMA
    strip = pltpu.VMEM((steps, fields, size, columns), jnp.bfloat16)
    column_strip = pltpu.VMEM((2, steps * fields, 16, depth), jnp.bfloat16)
    extra = max(lon_count.bit_length() - 3, 1)
    in_vmem = pl.BlockSpec(memory_space=pltpu.VMEM)
    bits = lon_count.bit_length() - 1
    advanced = pl.pallas_call(
        step_kernel,
        in_specs=[in_vmem] * 7,
        out_specs=in_vmem,
        out_shape=jax.ShapeDtypeStruct((fields, levels * rows, columns), jnp.float32),
        scratch_shapes=[
            pltpu.VMEM((columns, 2 * KC), jnp.bfloat16),
            pltpu.VMEM((2 * KC, columns), jnp.bfloat16),
            pltpu.VMEM((rows_each, columns), jnp.bfloat16),
            strip,
            strip,
            strip,
            strip,
            column_strip,
            column_strip,
            pltpu.VMEM((2, steps * fields, depth, 128), jnp.float32),
            pltpu.VMEM((steps, rows_each, 2 * KC), jnp.float32),
            pltpu.VMEM((steps, rows_each // 2, 2 * KC), jnp.float32),
            pltpu.VMEM((extra, steps, rows_each // 4, 2 * KC), jnp.float32),
            pltpu.VMEM((steps, rows_each // 2, 2 * KC), jnp.float32),
            pltpu.VMEM((bits - 1, steps, rows_each // 4, 2 * KC), jnp.float32),
            pltpu.VMEM((steps, rows_each, 2 * KC), jnp.bfloat16),
            dma((2, steps)),
            dma((2, steps)),
            dma((2,)),
            dma((2,)),
            dma((bits, steps)),
            dma((bits, steps)),
            dma((2, steps)),
            dma((2, steps)),
        ],
        compiler_params=pltpu.CompilerParams(
            collective_id=0, has_side_effects=True, vmem_limit_bytes=38 << 20
        ),
        name="step",
    )(
        state_fields.reshape(fields, levels * rows, columns),
        stencil_weights.reshape(4, levels * rows, columns),
        cosines,
        sines,
        turned_cosines,
        turned_sines,
        bounds,
    )
    return advanced.reshape(state_fields.shape)


def roots_table(columns, circle_size):
    steps = np.arange(columns)[:, None] * np.arange(KC)[None, :] % circle_size
    angles = steps * (2.0 * np.pi / circle_size)
    return np.concatenate([np.cos(angles), np.sin(angles)], axis=1).astype(jnp.bfloat16)


def quarter_turns(shape, axis, turns):
    phase = lax.rem(lax.broadcasted_iota(jnp.int32, shape, axis) * turns, 4)
    a = jnp.where(phase == 0, 1.0, jnp.where(phase == 2, -1.0, 0.0))
    b = jnp.where(phase == 1, 1.0, jnp.where(phase == 3, -1.0, 0.0))
    return a.astype(jnp.float32), b.astype(jnp.float32)


RELAYED = 4
FINISH = (0, 4, 1, 5, 2, 6, 3, 7)


def caps_kernel(
    state,
    weights,
    mask_in,
    cutoff_in,
    waves_in,
    turned_in,
    results,
    xs,
    ws,
    waves,
    turned,
    mask,
    cutoff,
    rounded,
    edges,
    halos,
    columns_out,
    columns_in,
    partial,
    half_in,
    coded,
    coded_in,
    passing,
    spectra,
    state_sem,
    weight_sem,
    table_sem,
    edge_send,
    edge_recv,
    column_send,
    column_recv,
    half_send,
    half_recv,
    code_send,
    code_recv,
    pass_send,
    pass_recv,
    join_send,
    join_recv,
):
    rows, fields, levels, columns = results.shape
    groups = levels // 8
    lines = fields * levels
    half = lines // 2
    lat_count, lon_count = lax.axis_size("lat"), lax.axis_size("lon")
    lat, lon = lax.axis_index("lat"), lax.axis_index("lon")
    after = lax.rem(lon + 1, lon_count)
    before = lax.rem(lon + lon_count - 1, lon_count)
    across = lax.rem(lon + lon_count // 2, lon_count)
    core = lax.rem(lon, 2)
    partner = lon + 1 - 2 * core
    circle_size = columns * lon_count
    first, last = lat == 0, lat == lat_count - 1
    polar = first | last
    middle = (lat == 2) | (lat == lat_count - 3)
    helper = jnp.where(first, 2, lat_count - 3)
    served = jnp.where(lat == 2, 0, lat_count - 1)
    edge_row = jnp.where(last, 0, rows - 1)

    def row_at(i):
        return jnp.where(i < rows - 2, i + 1, jnp.where(i == rows - 2, edge_row, rows - 1 - edge_row))

    own = pl.ds(pl.multiple_of(core * half, 16), half)
    other = pl.ds(pl.multiple_of((1 - core) * half, 16), half)

    def remote(source, target, sent, got, device):
        return pltpu.make_async_remote_copy(
            src_ref=source,
            dst_ref=target,
            send_sem=sent,
            recv_sem=got,
            device_id=device,
            device_id_type=MESH,
        )

    def state_copy(r):
        return pltpu.make_async_copy(state.at[:, :, r], xs.at[r + 1], state_sem.at[r])

    def weight_copy(r):
        return pltpu.make_async_copy(weights.at[:, :, r], ws.at[r], weight_sem.at[r])

    def table_copies():
        return (
            pltpu.make_async_copy(waves_in, waves, table_sem.at[0]),
            pltpu.make_async_copy(turned_in, turned, table_sem.at[1]),
        )

    def bound_copies():
        return (
            pltpu.make_async_copy(mask_in, mask, table_sem.at[2]),
            pltpu.make_async_copy(cutoff_in, cutoff, table_sem.at[3]),
        )

    def edge_copy(k, field, side, device):
        return remote(
            edges.at[k, field],
            halos.at[side, field],
            edge_send.at[k, field],
            edge_recv.at[side, field],
            device,
        )

    def column_copy(k, r, device):
        return remote(
            columns_out.at[k, r],
            columns_in.at[k, r],
            column_send.at[k, r],
            column_recv.at[k, r],
            device,
        )

    def half_copy(i):
        return remote(
            partial.at[i, other], half_in.at[i], half_send.at[i], half_recv.at[i], (lat, partner)
        )

    def code_copy(i):
        return remote(
            coded.at[i], coded_in.at[i], code_send.at[i], code_recv.at[i], (lat, across)
        )

    def lend_copy(i):
        return remote(
            coded.at[i], passing.at[i], code_send.at[i], pass_recv.at[i], (helper, across)
        )

    def pass_copy(i):
        return remote(
            passing.at[i], coded_in.at[i], pass_send.at[i], code_recv.at[i], (served, lon)
        )

    def join_copy(i):
        view = spectra.at[i, own]
        return remote(view, view, join_send.at[i], join_recv.at[i], (lat, partner))

    order = (0, rows - 1, *range(1, rows - 1))
    for r in order:
        state_copy(r).start()
    for copy in bound_copies():
        copy.start()
    for r in (*range(1, rows - 1), 0, rows - 1):
        weight_copy(r).start()

    @pl.when(polar)
    def _():
        for copy in table_copies():
            copy.start()

    barrier = pltpu.get_barrier_semaphore()

    def greet(a, b):
        pl.semaphore_signal(barrier, inc=1, device_id=(a, b), device_id_type=MESH)

    for b in (after, before, across):
        greet(lat, b)

    @pl.when(lat > 0)
    def _():
        greet(lat - 1, lon)

    @pl.when(lat < lat_count - 1)
    def _():
        greet(lat + 1, lon)

    @pl.when(polar)
    def _():
        greet(helper, lon)
        greet(helper, across)

    @pl.when(middle)
    def _():
        greet(served, lon)
        greet(served, across)

    for r in (0, rows - 1):
        state_copy(r).wait()
    for field in range(fields):
        sign = -1.0 if field < 2 else 1.0
        up_sign = jnp.where(first, sign, 1.0).astype(jnp.float32)
        down_sign = jnp.where(last, sign, 1.0).astype(jnp.float32)
        edges[0, field] = (xs[1, field] * up_sign).astype(jnp.bfloat16)
        edges[1, field] = (xs[rows, field] * down_sign).astype(jnp.bfloat16)

    @pl.when(polar)
    def _():
        pl.semaphore_wait(barrier, 3 + 1 + 2)

    @pl.when(middle)
    def _():
        pl.semaphore_wait(barrier, 3 + 2 + 2)

    @pl.when(jnp.logical_not(polar | middle))
    def _():
        pl.semaphore_wait(barrier, 3 + 2)

    for field in range(fields):

        @pl.when(lat > 0)
        def _():
            edge_copy(0, field, 1, (lat - 1, lon)).start()

        @pl.when(lat < lat_count - 1)
        def _():
            edge_copy(1, field, 0, (lat + 1, lon)).start()

    spot = lax.broadcasted_iota(jnp.int32, (8, 128), 1)

    def send_columns(r):
        to_after = jnp.zeros((8, 128), jnp.float32)
        to_before = jnp.zeros((8, 128), jnp.float32)
        for group in range(groups):
            for field in range(fields):
                at = group * fields + field
                span = pl.ds(group * 8, 8)
                right = xs[r + 1, field, span, pl.ds(columns - 128, 128)]
                left = xs[r + 1, field, span, pl.ds(0, 128)]
                to_after = jnp.where(spot == at, pltpu.roll(right, at + 1, 1), to_after)
                left = pltpu.roll(left, at, 1) if at else left
                to_before = jnp.where(spot == at, left, to_before)
        columns_out[0, r] = to_after
        columns_out[1, r] = to_before
        column_copy(0, r, (lat, after)).start()
        column_copy(1, r, (lat, before)).start()

    for j, r in enumerate((*range(1, rows - 1), rows - 1, 0)):
        if 0 < r < rows - 1:
            state_copy(r).wait()
        send_columns(r)
        if 1 <= j <= fields:

            @pl.when(first)
            def _():
                edge_copy(0, j - 1, 0, (lat, across)).start()

            @pl.when(last)
            def _():
                edge_copy(1, j - 1, 1, (lat, across)).start()

    for copy in bound_copies():
        copy.wait()

    @pl.when(polar)
    def _():
        for copy in table_copies():
            copy.wait()
        a, b = quarter_turns((16, KC), 1, lon)

        def turn_waves(t, carry):
            span = pl.ds(pl.multiple_of(t * 16, 16), 16)
            c = waves[span, :KC].astype(jnp.float32)
            s = waves[span, KC:].astype(jnp.float32)
            waves[span, :KC] = (a * c - b * s).astype(jnp.bfloat16)
            waves[span, KC:] = (a * s + b * c).astype(jnp.bfloat16)
            return carry

        lax.fori_loop(0, columns // 16, turn_waves, 0)
        u, v = quarter_turns((16, 128), 0, lon)

        def turn_back(t, carry):
            low = pl.ds(pl.multiple_of(t * 16, 16), 16)
            high = pl.ds(pl.multiple_of(KC + t * 16, 16), 16)
            for tile in range(columns // 128):
                lanes = pl.ds(tile * 128, 128)
                c = turned[low, lanes].astype(jnp.float32)
                s = turned[high, lanes].astype(jnp.float32)
                turned[low, lanes] = (u * c - v * s).astype(jnp.bfloat16)
                turned[high, lanes] = (u * s + v * c).astype(jnp.bfloat16)
            return carry

        lax.fori_loop(0, KC // 16, turn_back, 0)

    tiles = columns // 128

    def step(r):
        for group in range(groups):
            span = pl.ds(group * 8, 8)
            east_w, west_w, north_w, south_w = (ws[r, q, span] for q in range(4))
            for field in range(fields):
                at = group * fields + field
                x = xs[r + 1, field, span]
                n = xs[r, field, span]
                s = xs[r + 2, field, span]
                parts = [x[:, t * 128 : t * 128 + 128] for t in range(tiles)]
                left = columns_in[0, r]
                left = pltpu.roll(left, 128 - at, 1) if at else left
                right = pltpu.roll(columns_in[1, r], 127 - at, 1)
                right_turned = [left] + [pltpu.roll(p, 1, 1) for p in parts]
                left_turned = [pltpu.roll(p, 127, 1) for p in parts] + [right]
                w = jnp.concatenate(
                    [
                        jnp.where(spot == 0, right_turned[t], right_turned[t + 1])
                        for t in range(tiles)
                    ],
                    axis=1,
                )
                e = jnp.concatenate(
                    [
                        jnp.where(spot == 127, left_turned[t + 1], left_turned[t])
                        for t in range(tiles)
                    ],
                    axis=1,
                )
                y = (
                    x
                    + east_w * (e - x)
                    + west_w * (w - x)
                    + north_w * (n - x)
                    + south_w * (s - x)
                )
                results[r, field, span] = y

    def combine(i):
        half_copy(i).wait_recv()
        total = partial[i, own] + half_in[i]
        partial[i, own] = total
        largest = jnp.maximum(jnp.max(jnp.abs(total), axis=1, keepdims=True), 1e-30)
        power = jnp.ceil(jnp.log2(largest))
        code = jnp.round(total * (jnp.exp2(-power) * 32767.0))
        code = jnp.clip(code, -32767.0, 32767.0)
        place = lax.broadcasted_iota(jnp.int32, (half, 2 * KC), 1)
        code = jnp.where(place == KC, power, code)
        coded[i] = code.astype(jnp.int32).astype(jnp.int16)

    wave = lax.rem(lax.broadcasted_iota(jnp.int32, (8, 2 * KC), 1), KC)
    weight = jnp.where(wave == 0, 1.0 / circle_size, 2.0 / circle_size).astype(jnp.float32)

    def finish(i):
        code_copy(i).wait_recv()
        code = coded_in[i].astype(jnp.int32).astype(jnp.float32)
        unit = jnp.exp2(code[:, KC : KC + 1]) * (1.0 / 32767.0)
        place = lax.broadcasted_iota(jnp.int32, (half, 2 * KC), 1)
        code = jnp.where(place == KC, 0.0, code)
        total = partial[i, own] + code * unit
        limit = cutoff[lat * rows + row_at(i)]
        scale = jnp.where(wave <= limit, weight, 0.0)
        scaled = total.reshape(half // 8, 8, 2 * KC) * scale[None]
        spectra[i, own] = scaled.reshape(half, 2 * KC).astype(jnp.bfloat16)
        join_copy(i).start()

    def merge(i):
        join_copy(i).wait_recv()
        r = row_at(i)
        smooth = jnp.dot(spectra[i], turned[...], preferred_element_type=jnp.float32)
        smooth = smooth.astype(jnp.bfloat16).astype(jnp.float32)
        smooth = smooth.reshape(fields, levels, columns)
        kept = jnp.full((8, columns), mask[lat * rows + r], jnp.int32) != 0
        for field in range(fields):
            for group in range(groups):
                span = pl.ds(group * 8, 8)
                results[r, field, span] = jnp.where(
                    kept, smooth[field, group * 8 : group * 8 + 8], results[r, field, span]
                )

    def take_halo(side):
        for field in range(fields):
            edge_copy(0, field, side, (lat, across)).wait_recv()
        xs[side * (rows + 1)] = halos[side].astype(jnp.float32)

    def send_code(i):
        @pl.when(i < RELAYED)
        def _():
            lend_copy(i).start()

        @pl.when(i >= RELAYED)
        def _():
            code_copy(i).start()

    def advance(i, carry):
        r = row_at(i)

        @pl.when(i == rows - 2)
        def _():
            @pl.when(middle)
            def _():
                for p in range(RELAYED):
                    lend_copy(p).wait_recv()
                    pass_copy(p).start()

        @pl.when((i >= rows - 2) & (r == 0))
        def _():
            take_halo(0)

        @pl.when((i >= rows - 2) & (r == rows - 1))
        def _():
            take_halo(1)

        column_copy(0, r, (lat, after)).wait_recv()
        column_copy(1, r, (lat, before)).wait_recv()
        weight_copy(r).wait()
        step(r)

        @pl.when(polar)
        def _():
            rounded[...] = results[r].reshape(lines, columns).astype(jnp.bfloat16)
            partial[i] = jnp.dot(rounded[...], waves[...], preferred_element_type=jnp.float32)
            half_copy(i).start()

            @pl.when(i >= 1)
            def _():
                combine(i - 1)
                send_code(i - 1)

        return carry

    lax.fori_loop(0, rows, advance, 0)

    @pl.when(polar)
    def _():
        combine(rows - 1)
        send_code(rows - 1)

        def position(t):
            return t // 2 + (rows // 2) * lax.rem(t, 2)

        def endings(t, carry):
            finish(position(t))

            @pl.when(t >= 1)
            def _():
                merge(position(t - 1))

            return carry

        lax.fori_loop(0, rows, endings, 0)
        merge(position(rows - 1))

        def drain(i, carry):
            half_copy(i).wait_send()
            code_copy(i).wait_send()
            join_copy(i).wait_send()
            return carry

        lax.fori_loop(0, rows, drain, 0)

    @pl.when(middle)
    def _():
        for p in range(RELAYED):
            pass_copy(p).wait_send()

    for field in range(fields):
        for k in range(2):
            edge_copy(k, field, 0, (lat, across)).wait_send()
    for r in range(rows):
        for k in range(2):
            column_copy(k, r, (lat, after)).wait_send()


def place_kernel(stepped, out, sem):
    copies = [
        pltpu.make_async_copy(stepped.at[r], out.at[:, :, r], sem.at[r])
        for r in range(stepped.shape[0])
    ]
    for copy in copies:
        copy.start()
    for copy in copies:
        copy.wait()


def with_caps(state_fields, stencil_weights, filter_mask, cutoff_wave):
    fields, levels, rows, columns = state_fields.shape
    lon_count = lax.axis_size("lon")
    lines = fields * levels
    half = lines // 2
    table = roots_table(columns, columns * lon_count)
    dma = pltpu.SemaphoreType.DMA
    in_hbm = pl.BlockSpec(memory_space=pl.ANY)
    in_vmem = pl.BlockSpec(memory_space=pltpu.VMEM)
    f32, bf16, i16 = jnp.float32, jnp.bfloat16, jnp.int16
    stepped = pl.pallas_call(
        caps_kernel,
        in_specs=[in_hbm] * 6,
        out_specs=in_vmem,
        out_shape=jax.ShapeDtypeStruct((rows, fields, levels, columns), f32),
        scratch_shapes=[
            pltpu.VMEM((rows + 2, fields, levels, columns), f32),
            pltpu.VMEM((rows, 4, levels, columns), f32),
            pltpu.VMEM((columns, 2 * KC), bf16),
            pltpu.VMEM((2 * KC, columns), bf16),
            pltpu.SMEM(filter_mask.shape, jnp.int32),
            pltpu.SMEM(cutoff_wave.shape, jnp.int32),
            pltpu.VMEM((lines, columns), bf16),
            pltpu.VMEM((2, fields, levels, columns), bf16),
            pltpu.VMEM((2, fields, levels, columns), bf16),
            pltpu.VMEM((2, rows, 8, 128), f32),
            pltpu.VMEM((2, rows, 8, 128), f32),
            pltpu.VMEM((rows, lines, 2 * KC), f32),
            pltpu.VMEM((rows, half, 2 * KC), f32),
            pltpu.VMEM((rows, half, 2 * KC), i16),
            pltpu.VMEM((rows, half, 2 * KC), i16),
            pltpu.VMEM((RELAYED, half, 2 * KC), i16),
            pltpu.VMEM((rows, lines, 2 * KC), bf16),
            dma((rows,)),
            dma((rows,)),
            dma((4,)),
            dma((2, fields)),
            dma((2, fields)),
            dma((2, rows)),
            dma((2, rows)),
            dma((rows,)),
            dma((rows,)),
            dma((rows,)),
            dma((rows,)),
            dma((RELAYED,)),
            dma((RELAYED,)),
            dma((rows,)),
            dma((rows,)),
        ],
        compiler_params=pltpu.CompilerParams(
            collective_id=1, has_side_effects=True, vmem_limit_bytes=40_000_000
        ),
        name="caps",
    )(
        *(
            pltpu.with_memory_space_constraint(array, pltpu.HBM)
            for array in (
                state_fields,
                stencil_weights,
                filter_mask,
                cutoff_wave,
                jnp.asarray(table),
                jnp.asarray(np.ascontiguousarray(table.T)),
            )
        )
    )
    return pl.pallas_call(
        place_kernel,
        in_specs=[in_vmem],
        out_specs=in_hbm,
        out_shape=jax.ShapeDtypeStruct(state_fields.shape, f32),
        scratch_shapes=[dma((rows,))],
        compiler_params=pltpu.CompilerParams(vmem_limit_bytes=1 << 20),
        name="place",
    )(stepped)


def cap_rows(lat_rows):
    return {64: 8, 256: 40}.get(lat_rows, lat_rows)


def solution(mesh):
    def body(state_fields, stencil_weights, filter_mask, cutoff_wave):
        fields, levels, rows, columns = state_fields.shape
        one_block = cap_rows(filter_mask.shape[0]) <= rows
        suits = rows == 8 and columns % 128 == 0 and fields * levels % 32 == 0 and levels % 16 == 0
        if one_block and suits and mesh.shape["lon"] == 4 and mesh.shape["lat"] >= 6:
            return with_caps(state_fields, stencil_weights, filter_mask, cutoff_wave)
        return on_device(state_fields, stencil_weights, filter_mask, cutoff_wave)

    return jax.shard_map(
        body,
        mesh=mesh,
        in_specs=(P(None, None, "lat", "lon"), P(None, None, "lat", "lon"), P(), P()),
        out_specs=P(None, None, "lat", "lon"),
        check_vma=False,
    )
```

```python
import math

import jax
import jax.numpy as jnp
import numpy as np
from jax import lax
from jax.experimental import pallas as pl
from jax.experimental.pallas import tpu as pltpu
from jax.sharding import PartitionSpec as P

KC = 256


def angle_parts(columns, circle_size, axis):
    waves = lax.broadcasted_iota(
        jnp.int32, (columns.size, KC) if axis == 1 else (KC, columns.size), axis
    )
    product = jnp.expand_dims(columns, axis) * waves % circle_size
    angles = product.astype(jnp.float32) * (2.0 * math.pi / circle_size)
    return jnp.cos(angles), jnp.sin(angles)


MESH = pl.DeviceIdType.MESH


def step_kernel(
    state,
    weights,
    cosines,
    sines,
    turned_cosines,
    turned_sines,
    bounds,
    results,
    waves,
    turned,
    rounded,
    top,
    bottom,
    north,
    south,
    columns_out,
    columns_in,
    sides,
    partial,
    halves,
    quarters,
    half_in,
    quarter_in,
    spectra,
    row_send,
    row_recv,
    side_send,
    side_recv,
    sum_send,
    sum_recv,
    join_send,
    join_recv,
):
    fields, lines, columns = state.shape
    chunks, _, size, _ = top.shape
    depth = lines // chunks
    rows = depth // size
    modes = waves.shape[1] // 2
    half = partial.shape[1] // 2
    quarter = half // 2
    lat_count, lon_count = lax.axis_size("lat"), lax.axis_size("lon")
    lat, lon = lax.axis_index("lat"), lax.axis_index("lon")
    after = lax.rem(lon + 1, lon_count)
    before = lax.rem(lon + lon_count - 1, lon_count)
    across = lax.rem(lon + lon_count // 2, lon_count)
    bits = lon_count.bit_length() - 1
    digit = [lax.rem(lon // (1 << b), 2) for b in range(bits)]
    peer = [lon + (1 << b) - (2 << b) * digit[b] for b in range(bits)]
    own_half = digit[0] * half
    own_quarter = digit[1] * quarter

    def span_of(g, first, count):
        return pl.ds(pl.multiple_of(g * depth + first, count), count)

    def remote(source, target, sent, got, device):
        return pltpu.make_async_remote_copy(
            src_ref=source,
            dst_ref=target,
            send_sem=sent,
            recv_sem=got,
            device_id=device,
            device_id_type=MESH,
        )

    def row_copy(g, up, device, into_north):
        return remote(
            top.at[g] if up else bottom.at[g],
            north.at[g] if into_north else south.at[g],
            row_send.at[0 if up else 1, g],
            row_recv.at[0 if into_north else 1, g],
            device,
        )

    def side_copy(k, device):
        return remote(
            columns_out.at[k], columns_in.at[k], side_send.at[k], side_recv.at[k], device
        )

    def sum_copy(b, g):
        if b == 0:
            away = pl.ds(pl.multiple_of((1 - digit[0]) * half, 16), half)
            source, target = partial.at[g, away], half_in.at[g]
        elif b == 1:
            away = pl.ds(pl.multiple_of((1 - digit[1]) * quarter, 16), quarter)
            source, target = halves.at[g, away], quarter_in.at[0, g]
        else:
            source, target = quarters.at[b - 2, g], quarter_in.at[b - 1, g]
        return remote(source, target, sum_send.at[b, g], sum_recv.at[b, g], (lat, peer[b]))

    def join_copy(b, g):
        if b == 0:
            part = pl.ds(pl.multiple_of(own_half, 16), half)
        else:
            part = pl.ds(pl.multiple_of(own_half + own_quarter, 16), quarter)
        view = spectra.at[g, part]
        return remote(view, view, join_send.at[b, g], join_recv.at[b, g], (lat, peer[b]))

    barrier = pltpu.get_barrier_semaphore()
    for other in (after, before, across, *peer):
        pl.semaphore_signal(barrier, inc=1, device_id=(lat, other), device_id_type=MESH)

    @pl.when(lat > 0)
    def _():
        pl.semaphore_signal(barrier, inc=1, device_id=(lat - 1, lon), device_id_type=MESH)

    @pl.when(lat < lat_count - 1)
    def _():
        pl.semaphore_signal(barrier, inc=1, device_id=(lat + 1, lon), device_id_type=MESH)

    inside = (lat > 0) & (lat < lat_count - 1)

    @pl.when(inside)
    def _():
        pl.semaphore_wait(barrier, 5 + bits)

    @pl.when(jnp.logical_not(inside))
    def _():
        pl.semaphore_wait(barrier, 4 + bits)

    taker = lax.broadcasted_iota(jnp.int32, (2 * size, depth), 0)
    taken = lax.broadcasted_iota(jnp.int32, (2 * size, depth), 1)
    wanted = jnp.where(taker < size, taker * rows, (taker - size) * rows + rows - 1)
    gather = jnp.where(taken == wanted, 1.0, 0.0).astype(jnp.bfloat16)

    def send_rows(g, carry):
        for field in range(fields):
            sign = -1.0 if field < 2 else 1.0
            up_sign = jnp.where(lat == 0, sign, 1.0).astype(jnp.float32)
            down_sign = jnp.where(lat == lat_count - 1, sign, 1.0).astype(jnp.float32)
            edges = jnp.dot(
                gather,
                state[field, span_of(g, 0, depth)].astype(jnp.bfloat16),
                preferred_element_type=jnp.float32,
            )
            top[g, field] = (edges[:size] * up_sign).astype(jnp.bfloat16)
            bottom[g, field] = (edges[size:] * down_sign).astype(jnp.bfloat16)

        @pl.when(lat == 0)
        def _():
            row_copy(g, True, (lat, across), True).start()

        @pl.when(lat > 0)
        def _():
            row_copy(g, True, (lat - 1, lon), False).start()

        @pl.when(lat < lat_count - 1)
        def _():
            row_copy(g, False, (lat + 1, lon), True).start()

        @pl.when(lat == lat_count - 1)
        def _():
            row_copy(g, False, (lat, across), False).start()

        return carry

    lax.fori_loop(0, chunks, send_rows, 0)

    spot = lax.broadcasted_iota(jnp.int32, (16, 128), 1)
    line = lax.broadcasted_iota(jnp.int32, (16, 128), 0)

    def pick(k, lanes, lane):
        chosen = jnp.where((spot == lane) & (line == 0), 1.0, 0.0).astype(jnp.bfloat16)
        for g in range(chunks):
            for field in range(0, fields):
                first = (g * fields + field) * depth
                edge = state[field, span_of(g, 0, depth), lanes].astype(jnp.bfloat16)
                picked = lax.dot_general(
                    chosen, edge, (((1,), (1,)), ((), ())), preferred_element_type=jnp.float32
                )
                columns_out[k, g * fields + field] = picked.astype(jnp.bfloat16)

    pick(0, pl.ds(columns - 128, 128), 127)
    side_copy(0, (lat, after)).start()
    pick(1, pl.ds(0, 128), 0)
    side_copy(1, (lat, before)).start()

    fine = 32
    coarse = columns // fine
    fine_cos, fine_sin = cosines[coarse:], sines[coarse:]

    def fill(at, carry):
        span = pl.ds(pl.multiple_of(at * fine, fine), fine)
        coarse_cos, coarse_sin = cosines[pl.ds(at, 1)], sines[pl.ds(at, 1)]
        waves[span, :modes] = (coarse_cos * fine_cos - coarse_sin * fine_sin).astype(jnp.bfloat16)
        waves[span, modes:] = (coarse_sin * fine_cos + coarse_cos * fine_sin).astype(jnp.bfloat16)
        return carry

    lax.fori_loop(0, coarse, fill, 0)
    lane_cos, lane_sin = turned_cosines[:, :128], turned_sines[:, :128]
    for at in range(columns // 128):
        span = pl.ds(at * 128, 128)
        tile_cos = turned_cosines[:, 128 + at : 129 + at]
        tile_sin = turned_sines[:, 128 + at : 129 + at]
        turned[:modes, span] = (tile_cos * lane_cos - tile_sin * lane_sin).astype(jnp.bfloat16)
        turned[modes:, span] = (tile_sin * lane_cos + tile_cos * lane_sin).astype(jnp.bfloat16)

    spread = jnp.where(line == 0, 1.0, 0.0).astype(jnp.bfloat16)
    for k in range(2):
        side_copy(k, (lat, after)).wait_recv()
        for at in range(chunks * fields):
            sides[k, at] = lax.dot_general(
                columns_in[k, at],
                spread,
                (((0,), (0,)), ((), ())),
                preferred_element_type=jnp.float32,
            )

    lane = lax.broadcasted_iota(jnp.int32, (rows, columns), 1)
    level_line = lax.broadcasted_iota(jnp.int32, (rows, columns), 0)
    copies = columns // 128

    wave = lax.rem(lax.broadcasted_iota(jnp.int32, (rows, 2 * modes), 1), modes)
    circle_size = columns * lon_count
    weight = jnp.where(wave == 0, 1.0 / circle_size, 2.0 / circle_size)
    scale = jnp.where(wave <= bounds[:, 1:2], weight, 0.0).astype(jnp.float32)

    def advance(g):
        row_copy(g, True, (lat, across), True).wait_recv()
        row_copy(g, False, (lat, across), False).wait_recv()

        def one_field(field, inner):
            above = north[g, field].astype(jnp.float32)
            below = south[g, field].astype(jnp.float32)
            for level in range(0, size, 2):
                pair = []
                for at in (level, level + 1):
                    span = pl.ds(at * rows, rows)
                    here = span_of(g, at * rows, rows)
                    x = state[field, here]
                    left = jnp.concatenate([sides[0, g * fields + field, span]] * copies, axis=1)
                    right = jnp.concatenate([sides[1, g * fields + field, span]] * copies, axis=1)
                    w = jnp.where(lane == 0, left, pltpu.roll(x, 1, 1))
                    e = jnp.where(lane == columns - 1, right, pltpu.roll(x, columns - 1, 1))
                    n = jnp.where(level_line == 0, above[at : at + 1], pltpu.roll(x, 1, 0))
                    s = jnp.where(
                        level_line == rows - 1, below[at : at + 1], pltpu.roll(x, rows - 1, 0)
                    )
                    y = (
                        x
                        + weights[0, here] * (e - x)
                        + weights[1, here] * (w - x)
                        + weights[2, here] * (n - x)
                        + weights[3, here] * (s - x)
                    )
                    results[field, here] = y
                    pair.append(y)
                first = pl.multiple_of(field * depth + level * rows, 2 * rows)
                rounded[pl.ds(first, 2 * rows), :] = jnp.concatenate(pair, axis=0).astype(
                    jnp.bfloat16
                )
            return inner

        lax.fori_loop(0, fields, one_field, 0)
        partial[g] = jnp.dot(rounded[...], waves[...], preferred_element_type=jnp.float32)
        sum_copy(0, g).start()

    def pair_sum(g):
        sum_copy(0, g).wait_recv()
        mine = pl.ds(pl.multiple_of(own_half, 16), half)
        halves[g] = partial[g, mine] + half_in[g]
        sum_copy(1, g).start()

    def full_sum(g):
        sum_copy(1, g).wait_recv()
        mine = pl.ds(pl.multiple_of(own_quarter, 16), quarter)
        total = halves[g, mine] + quarter_in[0, g]
        for b in range(2, bits):
            quarters[b - 2, g] = total
            sum_copy(b, g).start()
            sum_copy(b, g).wait_recv()
            total = total + quarter_in[b - 1, g]
        scaled = total.reshape(quarter // rows, rows, 2 * modes) * scale[None]
        part = pl.ds(pl.multiple_of(own_half + own_quarter, 16), quarter)
        spectra[g, part] = scaled.reshape(quarter, 2 * modes).astype(jnp.bfloat16)
        join_copy(1, g).start()

    def join(g):
        join_copy(1, g).wait_recv()
        join_copy(0, g).start()

    def merge(g):
        join_copy(0, g).wait_recv()
        smooth = jnp.dot(spectra[g], turned[...], preferred_element_type=jnp.float32)
        smooth = smooth.astype(jnp.bfloat16).astype(jnp.float32)
        smooth = smooth.reshape(fields, size, rows, columns)
        kept = jnp.broadcast_to(bounds[:, 0:1], (rows, columns)) != 0
        for field in range(fields):
            for at in range(size):
                here = span_of(g, at * rows, rows)
                results[field, here] = jnp.where(kept, smooth[field, at], results[field, here])

    def forward(t, carry):
        advance(t)

        @pl.when(t >= 1)
        def _():
            pair_sum(t - 1)

        return carry

    last = chunks - 1
    lax.fori_loop(0, chunks, forward, 0)
    full_sum(0)
    pair_sum(last)

    def sums(g, carry):
        full_sum(g)
        return carry

    def joins(g, carry):
        join(g)
        return carry

    def merges(g, carry):
        merge(g)

        @pl.when(g + 2 < chunks)
        def _():
            join(g + 2)

        return carry

    lax.fori_loop(1, last, sums, 0)
    lax.fori_loop(0, 2, joins, 0)
    full_sum(last)
    lax.fori_loop(0, chunks, merges, 0)

    def finish(g, carry):
        for b in range(bits):
            sum_copy(b, g).wait_send()
        for b in range(2):
            join_copy(b, g).wait_send()
        row_copy(g, True, (lat, across), True).wait_send()
        row_copy(g, False, (lat, across), False).wait_send()
        return carry

    lax.fori_loop(0, chunks, finish, 0)
    for k in range(2):
        side_copy(k, (lat, after)).wait_send()


def on_device(state_fields, stencil_weights, filter_mask, cutoff_wave):
    fields, levels, rows, columns = state_fields.shape
    lat_count, lon_count = lax.axis_size("lat"), lax.axis_size("lon")
    lat_pos, lon_pos = lax.axis_index("lat"), lax.axis_index("lon")
    circle_size = columns * lon_count
    size = 8
    steps = levels // size
    start = lat_pos * rows
    bounds = lax.dynamic_slice_in_dim(jnp.stack([filter_mask, cutoff_wave], axis=1), start, rows)
    origin = lon_pos * columns
    cosines, sines = angle_parts(
        jnp.concatenate(
            [origin + 32 * jnp.arange(columns // 32), jnp.arange(32)]
        ).astype(jnp.int32),
        circle_size,
        1,
    )
    turned_cosines, turned_sines = angle_parts(
        jnp.concatenate(
            [jnp.arange(128), origin + 128 * jnp.arange(columns // 128)]
        ).astype(jnp.int32),
        circle_size,
        0,
    )
    rows_each = fields * size * rows
    depth = size * rows
    dma = pltpu.SemaphoreType.DMA
    strip = pltpu.VMEM((steps, fields, size, columns), jnp.bfloat16)
    column_strip = pltpu.VMEM((2, steps * fields, 16, depth), jnp.bfloat16)
    extra = max(lon_count.bit_length() - 3, 1)
    in_vmem = pl.BlockSpec(memory_space=pltpu.VMEM)
    bits = lon_count.bit_length() - 1
    advanced = pl.pallas_call(
        step_kernel,
        in_specs=[in_vmem] * 7,
        out_specs=in_vmem,
        out_shape=jax.ShapeDtypeStruct((fields, levels * rows, columns), jnp.float32),
        scratch_shapes=[
            pltpu.VMEM((columns, 2 * KC), jnp.bfloat16),
            pltpu.VMEM((2 * KC, columns), jnp.bfloat16),
            pltpu.VMEM((rows_each, columns), jnp.bfloat16),
            strip,
            strip,
            strip,
            strip,
            column_strip,
            column_strip,
            pltpu.VMEM((2, steps * fields, depth, 128), jnp.float32),
            pltpu.VMEM((steps, rows_each, 2 * KC), jnp.float32),
            pltpu.VMEM((steps, rows_each // 2, 2 * KC), jnp.float32),
            pltpu.VMEM((extra, steps, rows_each // 4, 2 * KC), jnp.float32),
            pltpu.VMEM((steps, rows_each // 2, 2 * KC), jnp.float32),
            pltpu.VMEM((bits - 1, steps, rows_each // 4, 2 * KC), jnp.float32),
            pltpu.VMEM((steps, rows_each, 2 * KC), jnp.bfloat16),
            dma((2, steps)),
            dma((2, steps)),
            dma((2,)),
            dma((2,)),
            dma((bits, steps)),
            dma((bits, steps)),
            dma((2, steps)),
            dma((2, steps)),
        ],
        compiler_params=pltpu.CompilerParams(
            collective_id=0, has_side_effects=True, vmem_limit_bytes=38 << 20
        ),
        name="step",
    )(
        state_fields.reshape(fields, levels * rows, columns),
        stencil_weights.reshape(4, levels * rows, columns),
        cosines,
        sines,
        turned_cosines,
        turned_sines,
        bounds,
    )
    return advanced.reshape(state_fields.shape)


def roots_table(columns, circle_size):
    steps = np.arange(columns)[:, None] * np.arange(KC)[None, :] % circle_size
    angles = steps * (2.0 * np.pi / circle_size)
    return np.concatenate([np.cos(angles), np.sin(angles)], axis=1).astype(jnp.bfloat16)


def quarter_turns(shape, axis, turns):
    phase = lax.rem(lax.broadcasted_iota(jnp.int32, shape, axis) * turns, 4)
    a = jnp.where(phase == 0, 1.0, jnp.where(phase == 2, -1.0, 0.0))
    b = jnp.where(phase == 1, 1.0, jnp.where(phase == 3, -1.0, 0.0))
    return a.astype(jnp.bfloat16), b.astype(jnp.bfloat16)


RELAYED = 4


def caps_kernel(
    state,
    weights,
    mask_in,
    cutoff_in,
    waves_in,
    turned_in,
    results,
    xs,
    ws,
    waves,
    turned,
    mask,
    cutoff,
    even_lines,
    odd_lines,
    edges,
    halos,
    columns_out,
    columns_in,
    partial,
    half_in,
    coded,
    coded_in,
    passing,
    spectra,
    state_sem,
    weight_sem,
    table_sem,
    edge_send,
    edge_recv,
    column_send,
    column_recv,
    half_send,
    half_recv,
    code_send,
    code_recv,
    pass_send,
    pass_recv,
    join_send,
    join_recv,
):
    rows, fields, levels, columns = results.shape
    groups = levels // 8
    lines = fields * levels
    half = lines // 2
    lat_count, lon_count = lax.axis_size("lat"), lax.axis_size("lon")
    lat, lon = lax.axis_index("lat"), lax.axis_index("lon")
    after = lax.rem(lon + 1, lon_count)
    before = lax.rem(lon + lon_count - 1, lon_count)
    across = lax.rem(lon + lon_count // 2, lon_count)
    core = lax.rem(lon, 2)
    partner = lon + 1 - 2 * core
    circle_size = columns * lon_count
    first, last = lat == 0, lat == lat_count - 1
    polar = first | last
    middle = (lat == 2) | (lat == lat_count - 3)
    helper = jnp.where(first, 2, lat_count - 3)
    served = jnp.where(lat == 2, 0, lat_count - 1)
    edge_row = jnp.where(last, 0, rows - 1)

    def row_at(i):
        return jnp.where(i < rows - 2, i + 1, jnp.where(i == rows - 2, edge_row, rows - 1 - edge_row))

    own = pl.ds(pl.multiple_of(core * half, 16), half)
    other = pl.ds(pl.multiple_of((1 - core) * half, 16), half)

    def remote(source, target, sent, got, device):
        return pltpu.make_async_remote_copy(
            src_ref=source,
            dst_ref=target,
            send_sem=sent,
            recv_sem=got,
            device_id=device,
            device_id_type=MESH,
        )

    def state_copy(r):
        return pltpu.make_async_copy(state.at[:, :, r], xs.at[r + 1], state_sem.at[r])

    def weight_copy(r):
        return pltpu.make_async_copy(weights.at[:, :, r], ws.at[r], weight_sem.at[r])

    def table_copies():
        return (
            pltpu.make_async_copy(waves_in, waves, table_sem.at[0]),
            pltpu.make_async_copy(turned_in, turned, table_sem.at[1]),
        )

    def bound_copies():
        return (
            pltpu.make_async_copy(mask_in, mask, table_sem.at[2]),
            pltpu.make_async_copy(cutoff_in, cutoff, table_sem.at[3]),
        )

    def edge_copy(k, field, side, device):
        return remote(
            edges.at[k, field],
            halos.at[side, field],
            edge_send.at[k],
            edge_recv.at[side, field],
            device,
        )

    def column_copy(k, r, device):
        return remote(
            columns_out.at[k, r],
            columns_in.at[k, r],
            column_send.at[k],
            column_recv.at[k, r],
            device,
        )

    def half_copy(i):
        return remote(
            partial.at[i, other], half_in.at[i], half_send.at[i], half_recv.at[i], (lat, partner)
        )

    def code_copy(i):
        return remote(
            coded.at[i], coded_in.at[i], code_send.at[i], code_recv.at[i], (lat, across)
        )

    def lend_copy(i):
        return remote(
            coded.at[i], passing.at[i], code_send.at[i], pass_recv.at[i], (helper, across)
        )

    def pass_copy(i):
        return remote(
            passing.at[i], coded_in.at[i], pass_send.at[i], code_recv.at[i], (served, lon)
        )

    def join_copy(i):
        view = spectra.at[i, own]
        return remote(view, view, join_send.at[i], join_recv.at[i], (lat, partner))

    for r in (0, rows - 1, *range(1, rows - 1)):
        state_copy(r).start()
    for copy in bound_copies():
        copy.start()
    for r in range(1, rows - 1):
        weight_copy(r).start()
        if r == 2:

            @pl.when(polar)
            def _():
                table_copies()[0].start()

    weight_copy(0).start()
    weight_copy(rows - 1).start()

    @pl.when(polar)
    def _():
        table_copies()[1].start()

    barrier = pltpu.get_barrier_semaphore()

    def greet(a, b):
        pl.semaphore_signal(barrier, inc=1, device_id=(a, b), device_id_type=MESH)

    for b in (after, before, across):
        greet(lat, b)

    @pl.when(lat > 0)
    def _():
        greet(lat - 1, lon)

    @pl.when(lat < lat_count - 1)
    def _():
        greet(lat + 1, lon)

    @pl.when(polar)
    def _():
        greet(helper, lon)
        greet(helper, across)

    @pl.when(middle)
    def _():
        greet(served, lon)
        greet(served, across)

    for r in (0, rows - 1):
        state_copy(r).wait()
    for field in range(fields):
        sign = -1.0 if field < 2 else 1.0
        up_sign = jnp.where(first, sign, 1.0).astype(jnp.float32)
        down_sign = jnp.where(last, sign, 1.0).astype(jnp.float32)
        edges[0, field] = (xs[1, field] * up_sign).astype(jnp.bfloat16)
        edges[1, field] = (xs[rows, field] * down_sign).astype(jnp.bfloat16)

    @pl.when(polar)
    def _():
        pl.semaphore_wait(barrier, 3 + 1 + 2)

    @pl.when(middle)
    def _():
        pl.semaphore_wait(barrier, 3 + 2 + 2)

    @pl.when(jnp.logical_not(polar | middle))
    def _():
        pl.semaphore_wait(barrier, 3 + 2)

    for field in range(fields):

        @pl.when(lat > 0)
        def _():
            edge_copy(0, field, 1, (lat - 1, lon)).start()

        @pl.when(lat < lat_count - 1)
        def _():
            edge_copy(1, field, 0, (lat + 1, lon)).start()

    spot = lax.broadcasted_iota(jnp.int32, (8, 128), 1)

    def send_columns(r):
        to_after = jnp.zeros((8, 128), jnp.float32)
        to_before = jnp.zeros((8, 128), jnp.float32)
        for group in range(groups):
            for field in range(fields):
                at = group * fields + field
                span = pl.ds(group * 8, 8)
                right = xs[r + 1, field, span, pl.ds(columns - 128, 128)]
                left = xs[r + 1, field, span, pl.ds(0, 128)]
                to_after = jnp.where(spot == at, pltpu.roll(right, at + 1, 1), to_after)
                left = pltpu.roll(left, at, 1) if at else left
                to_before = jnp.where(spot == at, left, to_before)
        columns_out[0, r] = to_after
        columns_out[1, r] = to_before
        column_copy(0, r, (lat, after)).start()
        column_copy(1, r, (lat, before)).start()

    for j, r in enumerate((*range(1, rows - 1), rows - 1, 0)):
        if 0 < r < rows - 1:
            state_copy(r).wait()
        send_columns(r)
        if 1 <= j <= fields:

            @pl.when(first)
            def _():
                edge_copy(0, j - 1, 0, (lat, across)).start()

            @pl.when(last)
            def _():
                edge_copy(1, j - 1, 1, (lat, across)).start()

    for copy in bound_copies():
        copy.wait()

    def turn_waves():
        table_copies()[0].wait()
        a, b = quarter_turns((16, KC), 1, lon)

        def turn(t, carry):
            for u in range(4):
                span = pl.ds(pl.multiple_of(t * 64 + u * 16, 16), 16)
                c, s = waves[span, :KC], waves[span, KC:]
                waves[span, :KC] = a * c - b * s
                waves[span, KC:] = a * s + b * c
            return carry

        lax.fori_loop(0, columns // 64, turn, 0)

    def turn_back():
        table_copies()[1].wait()
        a, b = quarter_turns((16, 128), 0, lon)

        def turn(t, carry):
            low = pl.ds(pl.multiple_of(t * 16, 16), 16)
            high = pl.ds(pl.multiple_of(KC + t * 16, 16), 16)
            for tile in range(columns // 128):
                lanes = pl.ds(tile * 128, 128)
                c, s = turned[low, lanes], turned[high, lanes]
                turned[low, lanes] = a * c - b * s
                turned[high, lanes] = a * s + b * c
            return carry

        lax.fori_loop(0, KC // 16, turn, 0)

    tiles = columns // 128

    def shares(r, group):
        span = pl.ds(group * 8, 8)
        return [ws[r, q, span] for q in range(4)]

    def advanced(r, field, group, east_w, west_w, north_w, south_w):
        at = group * fields + field
        span = pl.ds(group * 8, 8)
        x = xs[r + 1, field, span]
        n = xs[r, field, span]
        s = xs[r + 2, field, span]
        parts = [x[:, t * 128 : t * 128 + 128] for t in range(tiles)]
        left = columns_in[0, r]
        left = pltpu.roll(left, 128 - at, 1) if at else left
        right = pltpu.roll(columns_in[1, r], 127 - at, 1)
        to_right = [left] + [pltpu.roll(p, 1, 1) for p in parts]
        to_left = [pltpu.roll(p, 127, 1) for p in parts] + [right]
        w = [jnp.where(spot == 0, to_right[t], to_right[t + 1]) for t in range(tiles)]
        e = [jnp.where(spot == 127, to_left[t + 1], to_left[t]) for t in range(tiles)]
        y = (
            x
            + east_w * (jnp.concatenate(e, axis=1) - x)
            + west_w * (jnp.concatenate(w, axis=1) - x)
            + north_w * (n - x)
            + south_w * (s - x)
        )
        results[r, field, span] = y
        return y

    def ready(r):
        column_copy(0, r, (lat, after)).wait_recv()
        column_copy(1, r, (lat, before)).wait_recv()
        weight_copy(r).wait()

    def step(r):
        for group in range(groups):
            weight = shares(r, group)
            for field in range(fields):
                advanced(r, field, group, *weight)

    def step_into(r, target):
        for group in range(0, groups, 2):
            weight, next_weight = shares(r, group), shares(r, group + 1)
            for field in range(fields):
                pair = (
                    advanced(r, field, group, *weight),
                    advanced(r, field, group + 1, *next_weight),
                )
                target[pl.ds(field * levels + group * 8, 16)] = jnp.concatenate(
                    pair, axis=0
                ).astype(jnp.bfloat16)

    def transform(source, i):
        partial[i] = jnp.dot(source[...], waves[...], preferred_element_type=jnp.float32)

    def combine(i):
        half_copy(i).wait_recv()
        total = partial[i, own] + half_in[i]
        partial[i, own] = total
        largest = jnp.maximum(jnp.max(jnp.abs(total), axis=1, keepdims=True), 1e-30)
        power = jnp.ceil(jnp.log2(largest))
        code = jnp.round(total * (jnp.exp2(-power) * 32767.0))
        code = jnp.clip(code, -32767.0, 32767.0)
        place = lax.broadcasted_iota(jnp.int32, (half, 2 * KC), 1)
        code = jnp.where(place == KC, power, code)
        coded[i] = code.astype(jnp.int32).astype(jnp.int16)

    wave = lax.rem(lax.broadcasted_iota(jnp.int32, (8, 2 * KC), 1), KC)
    weight = jnp.where(wave == 0, 1.0 / circle_size, 2.0 / circle_size).astype(jnp.float32)

    def finish(i):
        code_copy(i).wait_recv()
        code = coded_in[i].astype(jnp.int32).astype(jnp.float32)
        unit = jnp.exp2(code[:, KC : KC + 1]) * (1.0 / 32767.0)
        place = lax.broadcasted_iota(jnp.int32, (half, 2 * KC), 1)
        code = jnp.where(place == KC, 0.0, code)
        total = partial[i, own] + code * unit
        limit = cutoff[lat * rows + row_at(i)]
        scale = jnp.where(wave <= limit, weight, 0.0)
        scaled = total.reshape(half // 8, 8, 2 * KC) * scale[None]
        spectra[i, own] = scaled.reshape(half, 2 * KC).astype(jnp.bfloat16)
        join_copy(i).start()

    def merge(i):
        join_copy(i).wait_recv()
        r = row_at(i)
        smooth = jnp.dot(spectra[i], turned[...], preferred_element_type=jnp.float32)
        smooth = smooth.astype(jnp.bfloat16).astype(jnp.float32)
        smooth = smooth.reshape(fields, levels, columns)
        kept = jnp.full((8, columns), mask[lat * rows + r], jnp.int32) != 0
        for field in range(fields):
            for group in range(groups):
                span = pl.ds(group * 8, 8)
                results[r, field, span] = jnp.where(
                    kept, smooth[field, group * 8 : group * 8 + 8], results[r, field, span]
                )

    def send_code(i):
        @pl.when(i < RELAYED)
        def _():
            lend_copy(i).start()

        @pl.when(i >= RELAYED)
        def _():
            code_copy(i).start()

    def combine_and_send(i):
        combine(i)
        send_code(i)

    pairs = (rows - 2) // 2

    @pl.when(polar)
    def _():
        turn_waves()
        odd_lines[...] = jnp.zeros_like(odd_lines)

        def two_rows(j, carry):
            i = 2 * j
            ready(i + 1)
            transform(odd_lines, jnp.where(j == 0, rows, i - 1))
            step_into(i + 1, even_lines)

            @pl.when(j >= 1)
            def _():
                half_copy(i - 1).start()

            @pl.when(j >= 2)
            def _():
                combine_and_send(i - 3)

            ready(i + 2)
            transform(even_lines, i)
            step_into(i + 2, odd_lines)
            half_copy(i).start()

            @pl.when(j >= 1)
            def _():
                combine_and_send(i - 2)

            return carry

        lax.fori_loop(0, pairs, two_rows, 0)
        transform(odd_lines, rows - 3)
        half_copy(rows - 3).start()
        combine_and_send(rows - 5)
        turn_back()
        combine_and_send(rows - 4)
        combine_and_send(rows - 3)

    @pl.when(jnp.logical_not(polar))
    def _():
        def one_row(r, carry):
            ready(r)
            step(r)
            return carry

        lax.fori_loop(1, rows - 1, one_row, 0)

    @pl.when(middle)
    def _():
        for p in range(RELAYED):
            lend_copy(p).wait_recv()
            pass_copy(p).start()

    ready(0)
    ready(rows - 1)
    for field in range(fields):
        for side, r in ((1, rows - 1), (0, 0)):
            edge_copy(0, field, side, (lat, across)).wait_recv()
            xs[side * (rows + 1), field] = halos[side, field].astype(jnp.float32)
            for group in range(groups):
                advanced(r, field, group, *shares(r, group))

    @pl.when(polar)
    def _():
        for i, lines_of in ((rows - 2, even_lines), (rows - 1, odd_lines)):
            r = row_at(i)
            lines_of[...] = results[r].reshape(lines, columns).astype(jnp.bfloat16)
            transform(lines_of, i)
            half_copy(i).start()
        combine_and_send(rows - 2)
        combine_and_send(rows - 1)

        def position(t):
            return t // 2 + (rows // 2) * (1 - lax.rem(t, 2))

        def endings(t, carry):
            finish(position(t))

            @pl.when(t >= 2)
            def _():
                merge(position(t - 2))

            return carry

        lax.fori_loop(0, rows, endings, 0)
        merge(position(rows - 2))
        merge(position(rows - 1))

        def drain(i, carry):
            half_copy(i).wait_send()
            code_copy(i).wait_send()
            join_copy(i).wait_send()
            return carry

        lax.fori_loop(0, rows, drain, 0)

    @pl.when(middle)
    def _():
        for p in range(RELAYED):
            pass_copy(p).wait_send()

    for k in range(2):
        remote(
            edges.at[k], halos.at[k], edge_send.at[k], edge_recv.at[k, 0], (lat, across)
        ).wait_send()
        remote(
            columns_out.at[k],
            columns_in.at[k],
            column_send.at[k],
            column_recv.at[k, 0],
            (lat, after),
        ).wait_send()


def place_kernel(stepped, out, sem):
    copies = [
        pltpu.make_async_copy(stepped.at[r], out.at[:, :, r], sem.at[r])
        for r in range(stepped.shape[0])
    ]
    for copy in copies:
        copy.start()
    for copy in copies:
        copy.wait()


def with_caps(state_fields, stencil_weights, filter_mask, cutoff_wave):
    fields, levels, rows, columns = state_fields.shape
    lon_count = lax.axis_size("lon")
    lines = fields * levels
    half = lines // 2
    table = roots_table(columns, columns * lon_count)
    dma = pltpu.SemaphoreType.DMA
    in_hbm = pl.BlockSpec(memory_space=pl.ANY)
    in_vmem = pl.BlockSpec(memory_space=pltpu.VMEM)
    f32, bf16, i16 = jnp.float32, jnp.bfloat16, jnp.int16
    stepped = pl.pallas_call(
        caps_kernel,
        in_specs=[in_hbm] * 6,
        out_specs=in_vmem,
        out_shape=jax.ShapeDtypeStruct((rows, fields, levels, columns), f32),
        scratch_shapes=[
            pltpu.VMEM((rows + 2, fields, levels, columns), f32),
            pltpu.VMEM((rows, 4, levels, columns), f32),
            pltpu.VMEM((columns, 2 * KC), bf16),
            pltpu.VMEM((2 * KC, columns), bf16),
            pltpu.SMEM(filter_mask.shape, jnp.int32),
            pltpu.SMEM(cutoff_wave.shape, jnp.int32),
            pltpu.VMEM((lines, columns), bf16),
            pltpu.VMEM((lines, columns), bf16),
            pltpu.VMEM((2, fields, levels, columns), bf16),
            pltpu.VMEM((2, fields, levels, columns), bf16),
            pltpu.VMEM((2, rows, 8, 128), f32),
            pltpu.VMEM((2, rows, 8, 128), f32),
            pltpu.VMEM((rows + 1, lines, 2 * KC), f32),
            pltpu.VMEM((rows, half, 2 * KC), f32),
            pltpu.VMEM((rows, half, 2 * KC), i16),
            pltpu.VMEM((rows, half, 2 * KC), i16),
            pltpu.VMEM((RELAYED, half, 2 * KC), i16),
            pltpu.VMEM((rows, lines, 2 * KC), bf16),
            dma((rows,)),
            dma((rows,)),
            dma((4,)),
            dma((2,)),
            dma((2, fields)),
            dma((2,)),
            dma((2, rows)),
            dma((rows,)),
            dma((rows,)),
            dma((rows,)),
            dma((rows,)),
            dma((RELAYED,)),
            dma((RELAYED,)),
            dma((rows,)),
            dma((rows,)),
        ],
        compiler_params=pltpu.CompilerParams(
            collective_id=1, has_side_effects=True, vmem_limit_bytes=40_000_000
        ),
        name="caps",
    )(
        *(
            pltpu.with_memory_space_constraint(array, pltpu.HBM)
            for array in (
                state_fields,
                stencil_weights,
                filter_mask,
                cutoff_wave,
                jnp.asarray(table),
                jnp.asarray(np.ascontiguousarray(table.T)),
            )
        )
    )
    return pl.pallas_call(
        place_kernel,
        in_specs=[in_vmem],
        out_specs=in_hbm,
        out_shape=jax.ShapeDtypeStruct(state_fields.shape, f32),
        scratch_shapes=[dma((rows,))],
        compiler_params=pltpu.CompilerParams(vmem_limit_bytes=1 << 20),
        name="place",
    )(stepped)


def cap_rows(lat_rows):
    return {64: 8, 256: 40}.get(lat_rows, lat_rows)


def solution(mesh):
    def body(state_fields, stencil_weights, filter_mask, cutoff_wave):
        fields, levels, rows, columns = state_fields.shape
        one_block = cap_rows(filter_mask.shape[0]) <= rows
        suits = rows == 8 and columns % 128 == 0 and fields * levels % 32 == 0 and levels % 16 == 0
        if one_block and suits and mesh.shape["lon"] == 4 and mesh.shape["lat"] >= 6:
            return with_caps(state_fields, stencil_weights, filter_mask, cutoff_wave)
        return on_device(state_fields, stencil_weights, filter_mask, cutoff_wave)

    return jax.shard_map(
        body,
        mesh=mesh,
        in_specs=(P(None, None, "lat", "lon"), P(None, None, "lat", "lon"), P(), P()),
        out_specs=P(None, None, "lat", "lon"),
        check_vma=False,
    )
```

```python
import math

import jax
import jax.numpy as jnp
import numpy as np
from jax import lax
from jax.experimental import pallas as pl
from jax.experimental.pallas import tpu as pltpu
from jax.sharding import PartitionSpec as P

KC = 256


def angle_parts(columns, circle_size, axis):
    waves = lax.broadcasted_iota(
        jnp.int32, (columns.size, KC) if axis == 1 else (KC, columns.size), axis
    )
    product = jnp.expand_dims(columns, axis) * waves % circle_size
    angles = product.astype(jnp.float32) * (2.0 * math.pi / circle_size)
    return jnp.cos(angles), jnp.sin(angles)


MESH = pl.DeviceIdType.MESH


def step_kernel(
    state,
    weights,
    cosines,
    sines,
    turned_cosines,
    turned_sines,
    bounds,
    results,
    waves,
    turned,
    rounded,
    top,
    bottom,
    north,
    south,
    columns_out,
    columns_in,
    sides,
    partial,
    halves,
    quarters,
    half_in,
    quarter_in,
    spectra,
    row_send,
    row_recv,
    side_send,
    side_recv,
    sum_send,
    sum_recv,
    join_send,
    join_recv,
):
    fields, lines, columns = state.shape
    chunks, _, size, _ = top.shape
    depth = lines // chunks
    rows = depth // size
    modes = waves.shape[1] // 2
    half = partial.shape[1] // 2
    quarter = half // 2
    lat_count, lon_count = lax.axis_size("lat"), lax.axis_size("lon")
    lat, lon = lax.axis_index("lat"), lax.axis_index("lon")
    after = lax.rem(lon + 1, lon_count)
    before = lax.rem(lon + lon_count - 1, lon_count)
    across = lax.rem(lon + lon_count // 2, lon_count)
    bits = lon_count.bit_length() - 1
    digit = [lax.rem(lon // (1 << b), 2) for b in range(bits)]
    peer = [lon + (1 << b) - (2 << b) * digit[b] for b in range(bits)]
    own_half = digit[0] * half
    own_quarter = digit[1] * quarter

    def span_of(g, first, count):
        return pl.ds(pl.multiple_of(g * depth + first, count), count)

    def remote(source, target, sent, got, device):
        return pltpu.make_async_remote_copy(
            src_ref=source,
            dst_ref=target,
            send_sem=sent,
            recv_sem=got,
            device_id=device,
            device_id_type=MESH,
        )

    def row_copy(g, up, device, into_north):
        return remote(
            top.at[g] if up else bottom.at[g],
            north.at[g] if into_north else south.at[g],
            row_send.at[0 if up else 1, g],
            row_recv.at[0 if into_north else 1, g],
            device,
        )

    def side_copy(k, device):
        return remote(
            columns_out.at[k], columns_in.at[k], side_send.at[k], side_recv.at[k], device
        )

    def sum_copy(b, g):
        if b == 0:
            away = pl.ds(pl.multiple_of((1 - digit[0]) * half, 16), half)
            source, target = partial.at[g, away], half_in.at[g]
        elif b == 1:
            away = pl.ds(pl.multiple_of((1 - digit[1]) * quarter, 16), quarter)
            source, target = halves.at[g, away], quarter_in.at[0, g]
        else:
            source, target = quarters.at[b - 2, g], quarter_in.at[b - 1, g]
        return remote(source, target, sum_send.at[b, g], sum_recv.at[b, g], (lat, peer[b]))

    def join_copy(b, g):
        if b == 0:
            part = pl.ds(pl.multiple_of(own_half, 16), half)
        else:
            part = pl.ds(pl.multiple_of(own_half + own_quarter, 16), quarter)
        view = spectra.at[g, part]
        return remote(view, view, join_send.at[b, g], join_recv.at[b, g], (lat, peer[b]))

    barrier = pltpu.get_barrier_semaphore()
    for other in (after, before, across, *peer):
        pl.semaphore_signal(barrier, inc=1, device_id=(lat, other), device_id_type=MESH)

    @pl.when(lat > 0)
    def _():
        pl.semaphore_signal(barrier, inc=1, device_id=(lat - 1, lon), device_id_type=MESH)

    @pl.when(lat < lat_count - 1)
    def _():
        pl.semaphore_signal(barrier, inc=1, device_id=(lat + 1, lon), device_id_type=MESH)

    inside = (lat > 0) & (lat < lat_count - 1)

    @pl.when(inside)
    def _():
        pl.semaphore_wait(barrier, 5 + bits)

    @pl.when(jnp.logical_not(inside))
    def _():
        pl.semaphore_wait(barrier, 4 + bits)

    taker = lax.broadcasted_iota(jnp.int32, (2 * size, depth), 0)
    taken = lax.broadcasted_iota(jnp.int32, (2 * size, depth), 1)
    wanted = jnp.where(taker < size, taker * rows, (taker - size) * rows + rows - 1)
    gather = jnp.where(taken == wanted, 1.0, 0.0).astype(jnp.bfloat16)

    def send_rows(g, carry):
        for field in range(fields):
            sign = -1.0 if field < 2 else 1.0
            up_sign = jnp.where(lat == 0, sign, 1.0).astype(jnp.float32)
            down_sign = jnp.where(lat == lat_count - 1, sign, 1.0).astype(jnp.float32)
            edges = jnp.dot(
                gather,
                state[field, span_of(g, 0, depth)].astype(jnp.bfloat16),
                preferred_element_type=jnp.float32,
            )
            top[g, field] = (edges[:size] * up_sign).astype(jnp.bfloat16)
            bottom[g, field] = (edges[size:] * down_sign).astype(jnp.bfloat16)

        @pl.when(lat == 0)
        def _():
            row_copy(g, True, (lat, across), True).start()

        @pl.when(lat > 0)
        def _():
            row_copy(g, True, (lat - 1, lon), False).start()

        @pl.when(lat < lat_count - 1)
        def _():
            row_copy(g, False, (lat + 1, lon), True).start()

        @pl.when(lat == lat_count - 1)
        def _():
            row_copy(g, False, (lat, across), False).start()

        return carry

    lax.fori_loop(0, chunks, send_rows, 0)

    spot = lax.broadcasted_iota(jnp.int32, (16, 128), 1)
    line = lax.broadcasted_iota(jnp.int32, (16, 128), 0)

    def pick(k, lanes, lane):
        chosen = jnp.where((spot == lane) & (line == 0), 1.0, 0.0).astype(jnp.bfloat16)
        for g in range(chunks):
            for field in range(0, fields):
                first = (g * fields + field) * depth
                edge = state[field, span_of(g, 0, depth), lanes].astype(jnp.bfloat16)
                picked = lax.dot_general(
                    chosen, edge, (((1,), (1,)), ((), ())), preferred_element_type=jnp.float32
                )
                columns_out[k, g * fields + field] = picked.astype(jnp.bfloat16)

    pick(0, pl.ds(columns - 128, 128), 127)
    side_copy(0, (lat, after)).start()
    pick(1, pl.ds(0, 128), 0)
    side_copy(1, (lat, before)).start()

    fine = 32
    coarse = columns // fine
    fine_cos, fine_sin = cosines[coarse:], sines[coarse:]

    def fill(at, carry):
        span = pl.ds(pl.multiple_of(at * fine, fine), fine)
        coarse_cos, coarse_sin = cosines[pl.ds(at, 1)], sines[pl.ds(at, 1)]
        waves[span, :modes] = (coarse_cos * fine_cos - coarse_sin * fine_sin).astype(jnp.bfloat16)
        waves[span, modes:] = (coarse_sin * fine_cos + coarse_cos * fine_sin).astype(jnp.bfloat16)
        return carry

    lax.fori_loop(0, coarse, fill, 0)
    lane_cos, lane_sin = turned_cosines[:, :128], turned_sines[:, :128]
    for at in range(columns // 128):
        span = pl.ds(at * 128, 128)
        tile_cos = turned_cosines[:, 128 + at : 129 + at]
        tile_sin = turned_sines[:, 128 + at : 129 + at]
        turned[:modes, span] = (tile_cos * lane_cos - tile_sin * lane_sin).astype(jnp.bfloat16)
        turned[modes:, span] = (tile_sin * lane_cos + tile_cos * lane_sin).astype(jnp.bfloat16)

    spread = jnp.where(line == 0, 1.0, 0.0).astype(jnp.bfloat16)
    for k in range(2):
        side_copy(k, (lat, after)).wait_recv()
        for at in range(chunks * fields):
            sides[k, at] = lax.dot_general(
                columns_in[k, at],
                spread,
                (((0,), (0,)), ((), ())),
                preferred_element_type=jnp.float32,
            )

    lane = lax.broadcasted_iota(jnp.int32, (rows, columns), 1)
    level_line = lax.broadcasted_iota(jnp.int32, (rows, columns), 0)
    copies = columns // 128

    wave = lax.rem(lax.broadcasted_iota(jnp.int32, (rows, 2 * modes), 1), modes)
    circle_size = columns * lon_count
    weight = jnp.where(wave == 0, 1.0 / circle_size, 2.0 / circle_size)
    scale = jnp.where(wave <= bounds[:, 1:2], weight, 0.0).astype(jnp.float32)

    def advance(g):
        row_copy(g, True, (lat, across), True).wait_recv()
        row_copy(g, False, (lat, across), False).wait_recv()

        def one_field(field, inner):
            above = north[g, field].astype(jnp.float32)
            below = south[g, field].astype(jnp.float32)
            for level in range(0, size, 2):
                pair = []
                for at in (level, level + 1):
                    span = pl.ds(at * rows, rows)
                    here = span_of(g, at * rows, rows)
                    x = state[field, here]
                    left = jnp.concatenate([sides[0, g * fields + field, span]] * copies, axis=1)
                    right = jnp.concatenate([sides[1, g * fields + field, span]] * copies, axis=1)
                    w = jnp.where(lane == 0, left, pltpu.roll(x, 1, 1))
                    e = jnp.where(lane == columns - 1, right, pltpu.roll(x, columns - 1, 1))
                    n = jnp.where(level_line == 0, above[at : at + 1], pltpu.roll(x, 1, 0))
                    s = jnp.where(
                        level_line == rows - 1, below[at : at + 1], pltpu.roll(x, rows - 1, 0)
                    )
                    y = (
                        x
                        + weights[0, here] * (e - x)
                        + weights[1, here] * (w - x)
                        + weights[2, here] * (n - x)
                        + weights[3, here] * (s - x)
                    )
                    results[field, here] = y
                    pair.append(y)
                first = pl.multiple_of(field * depth + level * rows, 2 * rows)
                rounded[pl.ds(first, 2 * rows), :] = jnp.concatenate(pair, axis=0).astype(
                    jnp.bfloat16
                )
            return inner

        lax.fori_loop(0, fields, one_field, 0)
        partial[g] = jnp.dot(rounded[...], waves[...], preferred_element_type=jnp.float32)
        sum_copy(0, g).start()

    def pair_sum(g):
        sum_copy(0, g).wait_recv()
        mine = pl.ds(pl.multiple_of(own_half, 16), half)
        halves[g] = partial[g, mine] + half_in[g]
        sum_copy(1, g).start()

    def full_sum(g):
        sum_copy(1, g).wait_recv()
        mine = pl.ds(pl.multiple_of(own_quarter, 16), quarter)
        total = halves[g, mine] + quarter_in[0, g]
        for b in range(2, bits):
            quarters[b - 2, g] = total
            sum_copy(b, g).start()
            sum_copy(b, g).wait_recv()
            total = total + quarter_in[b - 1, g]
        scaled = total.reshape(quarter // rows, rows, 2 * modes) * scale[None]
        part = pl.ds(pl.multiple_of(own_half + own_quarter, 16), quarter)
        spectra[g, part] = scaled.reshape(quarter, 2 * modes).astype(jnp.bfloat16)
        join_copy(1, g).start()

    def join(g):
        join_copy(1, g).wait_recv()
        join_copy(0, g).start()

    def merge(g):
        join_copy(0, g).wait_recv()
        smooth = jnp.dot(spectra[g], turned[...], preferred_element_type=jnp.float32)
        smooth = smooth.astype(jnp.bfloat16).astype(jnp.float32)
        smooth = smooth.reshape(fields, size, rows, columns)
        kept = jnp.broadcast_to(bounds[:, 0:1], (rows, columns)) != 0
        for field in range(fields):
            for at in range(size):
                here = span_of(g, at * rows, rows)
                results[field, here] = jnp.where(kept, smooth[field, at], results[field, here])

    def forward(t, carry):
        advance(t)

        @pl.when(t >= 1)
        def _():
            pair_sum(t - 1)

        return carry

    last = chunks - 1
    lax.fori_loop(0, chunks, forward, 0)
    full_sum(0)
    pair_sum(last)

    def sums(g, carry):
        full_sum(g)
        return carry

    def joins(g, carry):
        join(g)
        return carry

    def merges(g, carry):
        merge(g)

        @pl.when(g + 2 < chunks)
        def _():
            join(g + 2)

        return carry

    lax.fori_loop(1, last, sums, 0)
    lax.fori_loop(0, 2, joins, 0)
    full_sum(last)
    lax.fori_loop(0, chunks, merges, 0)

    def finish(g, carry):
        for b in range(bits):
            sum_copy(b, g).wait_send()
        for b in range(2):
            join_copy(b, g).wait_send()
        row_copy(g, True, (lat, across), True).wait_send()
        row_copy(g, False, (lat, across), False).wait_send()
        return carry

    lax.fori_loop(0, chunks, finish, 0)
    for k in range(2):
        side_copy(k, (lat, after)).wait_send()


def on_device(state_fields, stencil_weights, filter_mask, cutoff_wave):
    fields, levels, rows, columns = state_fields.shape
    lat_count, lon_count = lax.axis_size("lat"), lax.axis_size("lon")
    lat_pos, lon_pos = lax.axis_index("lat"), lax.axis_index("lon")
    circle_size = columns * lon_count
    size = 8
    steps = levels // size
    start = lat_pos * rows
    bounds = lax.dynamic_slice_in_dim(jnp.stack([filter_mask, cutoff_wave], axis=1), start, rows)
    origin = lon_pos * columns
    cosines, sines = angle_parts(
        jnp.concatenate(
            [origin + 32 * jnp.arange(columns // 32), jnp.arange(32)]
        ).astype(jnp.int32),
        circle_size,
        1,
    )
    turned_cosines, turned_sines = angle_parts(
        jnp.concatenate(
            [jnp.arange(128), origin + 128 * jnp.arange(columns // 128)]
        ).astype(jnp.int32),
        circle_size,
        0,
    )
    rows_each = fields * size * rows
    depth = size * rows
    dma = pltpu.SemaphoreType.DMA
    strip = pltpu.VMEM((steps, fields, size, columns), jnp.bfloat16)
    column_strip = pltpu.VMEM((2, steps * fields, 16, depth), jnp.bfloat16)
    extra = max(lon_count.bit_length() - 3, 1)
    in_vmem = pl.BlockSpec(memory_space=pltpu.VMEM)
    bits = lon_count.bit_length() - 1
    advanced = pl.pallas_call(
        step_kernel,
        in_specs=[in_vmem] * 7,
        out_specs=in_vmem,
        out_shape=jax.ShapeDtypeStruct((fields, levels * rows, columns), jnp.float32),
        scratch_shapes=[
            pltpu.VMEM((columns, 2 * KC), jnp.bfloat16),
            pltpu.VMEM((2 * KC, columns), jnp.bfloat16),
            pltpu.VMEM((rows_each, columns), jnp.bfloat16),
            strip,
            strip,
            strip,
            strip,
            column_strip,
            column_strip,
            pltpu.VMEM((2, steps * fields, depth, 128), jnp.float32),
            pltpu.VMEM((steps, rows_each, 2 * KC), jnp.float32),
            pltpu.VMEM((steps, rows_each // 2, 2 * KC), jnp.float32),
            pltpu.VMEM((extra, steps, rows_each // 4, 2 * KC), jnp.float32),
            pltpu.VMEM((steps, rows_each // 2, 2 * KC), jnp.float32),
            pltpu.VMEM((bits - 1, steps, rows_each // 4, 2 * KC), jnp.float32),
            pltpu.VMEM((steps, rows_each, 2 * KC), jnp.bfloat16),
            dma((2, steps)),
            dma((2, steps)),
            dma((2,)),
            dma((2,)),
            dma((bits, steps)),
            dma((bits, steps)),
            dma((2, steps)),
            dma((2, steps)),
        ],
        compiler_params=pltpu.CompilerParams(
            collective_id=0, has_side_effects=True, vmem_limit_bytes=38 << 20
        ),
        name="step",
    )(
        state_fields.reshape(fields, levels * rows, columns),
        stencil_weights.reshape(4, levels * rows, columns),
        cosines,
        sines,
        turned_cosines,
        turned_sines,
        bounds,
    )
    return advanced.reshape(state_fields.shape)


def roots_table(columns, circle_size):
    steps = np.arange(columns)[:, None] * np.arange(KC)[None, :] % circle_size
    angles = steps * (2.0 * np.pi / circle_size)
    return np.concatenate([np.cos(angles), np.sin(angles)], axis=1).astype(jnp.bfloat16)


def quarter_turns(shape, axis, turns):
    phase = lax.rem(lax.broadcasted_iota(jnp.int32, shape, axis) * turns, 4)
    a = jnp.where(phase == 0, 1.0, jnp.where(phase == 2, -1.0, 0.0))
    b = jnp.where(phase == 1, 1.0, jnp.where(phase == 3, -1.0, 0.0))
    return a.astype(jnp.bfloat16), b.astype(jnp.bfloat16)


RELAYED = 3


def caps_kernel(
    state,
    weights,
    mask_in,
    cutoff_in,
    waves_in,
    turned_in,
    results,
    xs,
    ws,
    waves,
    turned,
    mask,
    cutoff,
    even_lines,
    odd_lines,
    edges,
    halos,
    columns_out,
    columns_in,
    partial,
    half_in,
    coded,
    coded_in,
    passing,
    spectra,
    state_sem,
    weight_sem,
    table_sem,
    edge_send,
    edge_recv,
    column_send,
    column_recv,
    half_send,
    half_recv,
    code_send,
    code_recv,
    lend_send,
    lend_recv,
    pass_send,
    pass_recv,
    join_send,
    join_recv,
):
    rows, fields, levels, columns = results.shape
    groups = levels // 8
    lines = fields * levels
    half = lines // 2
    lat_count, lon_count = lax.axis_size("lat"), lax.axis_size("lon")
    lat, lon = lax.axis_index("lat"), lax.axis_index("lon")
    after = lax.rem(lon + 1, lon_count)
    before = lax.rem(lon + lon_count - 1, lon_count)
    across = lax.rem(lon + lon_count // 2, lon_count)
    core = lax.rem(lon, 2)
    partner = lon + 1 - 2 * core
    circle_size = columns * lon_count
    first, last = lat == 0, lat == lat_count - 1
    polar = first | last
    middle = (lat == 2) | (lat == lat_count - 3)
    helper = jnp.where(first, 2, lat_count - 3)
    served = jnp.where(lat == 2, 0, lat_count - 1)
    edge_row = jnp.where(last, 0, rows - 1)

    def row_at(i):
        return jnp.where(i < rows - 2, i + 1, jnp.where(i == rows - 2, edge_row, rows - 1 - edge_row))

    own = pl.ds(pl.multiple_of(core * half, 16), half)
    other = pl.ds(pl.multiple_of((1 - core) * half, 16), half)

    def remote(source, target, sent, got, device):
        return pltpu.make_async_remote_copy(
            src_ref=source,
            dst_ref=target,
            send_sem=sent,
            recv_sem=got,
            device_id=device,
            device_id_type=MESH,
        )

    def state_copy(r):
        return pltpu.make_async_copy(state.at[:, :, r], xs.at[r + 1], state_sem.at[r])

    def weight_copy(r):
        return pltpu.make_async_copy(weights.at[:, :, r], ws.at[r], weight_sem.at[r])

    def table_copies():
        return (
            pltpu.make_async_copy(waves_in.at[core], waves, table_sem.at[0]),
            pltpu.make_async_copy(turned_in, turned, table_sem.at[1]),
        )

    def bound_copies():
        return (
            pltpu.make_async_copy(mask_in, mask, table_sem.at[2]),
            pltpu.make_async_copy(cutoff_in, cutoff, table_sem.at[3]),
        )

    def edge_copy(k, field, side, device):
        return remote(
            edges.at[k, field],
            halos.at[side, field],
            edge_send.at[k],
            edge_recv.at[side, field],
            device,
        )

    def column_copy(k, r, device):
        return remote(
            columns_out.at[k, r],
            columns_in.at[k, r],
            column_send.at[k],
            column_recv.at[k, r],
            device,
        )

    def half_copy(i):
        return remote(
            partial.at[i, other], half_in.at[i], half_send.at[i], half_recv.at[i], (lat, partner)
        )

    def code_copy(i):
        return remote(
            coded.at[i], coded_in.at[i], code_send.at[i], code_recv.at[i], (lat, across)
        )

    first_piece = (half // 2 + 15) // 16 * 16
    pieces = (pl.ds(0, first_piece), pl.ds(first_piece, half - first_piece))

    def lend_copy(i, k):
        return remote(
            coded.at[i, pieces[k]],
            passing.at[i, pieces[k]],
            lend_send.at[i, k],
            pass_recv.at[i, k],
            (helper, across),
        )

    def pass_copy(i, k):
        return remote(
            passing.at[i, pieces[k]],
            coded_in.at[i, pieces[k]],
            pass_send.at[i, k],
            lend_recv.at[i, k],
            (served, lon),
        )

    def join_copy(i):
        view = spectra.at[i, own]
        return remote(view, view, join_send.at[i], join_recv.at[i], (lat, partner))

    barrier = pltpu.get_barrier_semaphore()

    def greet(a, b):
        pl.semaphore_signal(barrier, inc=1, device_id=(a, b), device_id_type=MESH)

    for b in (after, before, across):
        greet(lat, b)

    @pl.when(lat > 0)
    def _():
        greet(lat - 1, lon)

    @pl.when(lat < lat_count - 1)
    def _():
        greet(lat + 1, lon)

    @pl.when(polar)
    def _():
        greet(helper, lon)
        greet(helper, across)

    @pl.when(middle)
    def _():
        greet(served, lon)
        greet(served, across)

    for r in (0, rows - 1, *range(1, rows - 1)):
        state_copy(r).start()

    @pl.when(polar)
    def _():
        table_copies()[0].start()

    for copy in bound_copies():
        copy.start()
    for r in (*range(1, rows - 1), 0, rows - 1):
        weight_copy(r).start()

    @pl.when(polar)
    def _():
        table_copies()[1].start()

    for r in (0, rows - 1):
        state_copy(r).wait()
    for field in range(fields):
        sign = -1.0 if field < 2 else 1.0
        up_sign = jnp.where(first, sign, 1.0).astype(jnp.float32)
        down_sign = jnp.where(last, sign, 1.0).astype(jnp.float32)
        edges[0, field] = (xs[1, field] * up_sign).astype(jnp.bfloat16)
        edges[1, field] = (xs[rows, field] * down_sign).astype(jnp.bfloat16)

    @pl.when(polar)
    def _():
        pl.semaphore_wait(barrier, 3 + 1 + 2)

    @pl.when(middle)
    def _():
        pl.semaphore_wait(barrier, 3 + 2 + 2)

    @pl.when(jnp.logical_not(polar | middle))
    def _():
        pl.semaphore_wait(barrier, 3 + 2)

    def send_up(field):
        @pl.when(lat > 0)
        def _():
            edge_copy(0, field, 1, (lat - 1, lon)).start()

    def send_down(field):
        @pl.when(lat < lat_count - 1)
        def _():
            edge_copy(1, field, 0, (lat + 1, lon)).start()

    beside_first, beside_last = lat == 1, lat == lat_count - 2

    @pl.when(beside_first)
    def _():
        for field in range(fields):
            send_up(field)
        for field in range(fields):
            send_down(field)

    @pl.when(beside_last)
    def _():
        for field in range(fields):
            send_down(field)
        for field in range(fields):
            send_up(field)

    @pl.when(jnp.logical_not(beside_first | beside_last))
    def _():
        for field in range(fields):
            send_up(field)
            send_down(field)

    spot = lax.broadcasted_iota(jnp.int32, (8, 128), 1)

    def send_columns(r):
        to_after = jnp.zeros((8, 128), jnp.float32)
        to_before = jnp.zeros((8, 128), jnp.float32)
        for group in range(groups):
            for field in range(fields):
                at = group * fields + field
                span = pl.ds(group * 8, 8)
                right = xs[r + 1, field, span, pl.ds(columns - 128, 128)]
                left = xs[r + 1, field, span, pl.ds(0, 128)]
                to_after = jnp.where(spot == at, pltpu.roll(right, at + 1, 1), to_after)
                left = pltpu.roll(left, at, 1) if at else left
                to_before = jnp.where(spot == at, left, to_before)
        columns_out[0, r] = to_after
        columns_out[1, r] = to_before
        column_copy(0, r, (lat, after)).start()
        column_copy(1, r, (lat, before)).start()

    def send_rim(field):
        @pl.when(first)
        def _():
            edge_copy(0, field, 0, (lat, across)).start()

        @pl.when(last)
        def _():
            edge_copy(1, field, 1, (lat, across)).start()

    for r in (*range(1, rows - 1), rows - 1, 0):
        if 0 < r < rows - 1:
            state_copy(r).wait()
        send_columns(r)
        if r == 3:
            send_rim(0)
    for field in range(1, fields):
        send_rim(field)

    for copy in bound_copies():
        copy.wait()

    def turn_back():
        table_copies()[1].wait()
        a, b = quarter_turns((16, 128), 0, core)

        def turn(t, carry):
            low = pl.ds(pl.multiple_of(t * 16, 16), 16)
            high = pl.ds(pl.multiple_of(KC + t * 16, 16), 16)
            for tile in range(columns // 128):
                lanes = pl.ds(tile * 128, 128)
                c, s = turned[low, lanes], turned[high, lanes]
                turned[low, lanes] = a * c - b * s
                turned[high, lanes] = a * s + b * c
            return carry

        lax.fori_loop(0, KC // 16, turn, 0)

    tiles = columns // 128

    def shares(r, group):
        span = pl.ds(group * 8, 8)
        return [ws[r, q, span] for q in range(4)]

    def advanced(r, field, group, east_w, west_w, north_w, south_w):
        at = group * fields + field
        span = pl.ds(group * 8, 8)
        x = xs[r + 1, field, span]
        n = xs[r, field, span]
        s = xs[r + 2, field, span]
        parts = [x[:, t * 128 : t * 128 + 128] for t in range(tiles)]
        left = columns_in[0, r]
        left = pltpu.roll(left, 128 - at, 1) if at else left
        right = pltpu.roll(columns_in[1, r], 127 - at, 1)
        to_right = [left] + [pltpu.roll(p, 1, 1) for p in parts]
        to_left = [pltpu.roll(p, 127, 1) for p in parts] + [right]
        w = [jnp.where(spot == 0, to_right[t], to_right[t + 1]) for t in range(tiles)]
        e = [jnp.where(spot == 127, to_left[t + 1], to_left[t]) for t in range(tiles)]
        y = (
            x
            + east_w * (jnp.concatenate(e, axis=1) - x)
            + west_w * (jnp.concatenate(w, axis=1) - x)
            + north_w * (n - x)
            + south_w * (s - x)
        )
        results[r, field, span] = y
        return y

    def ready(r):
        column_copy(0, r, (lat, after)).wait_recv()
        column_copy(1, r, (lat, before)).wait_recv()
        weight_copy(r).wait()

    def step(r):
        for group in range(groups):
            weight = shares(r, group)
            for field in range(fields):
                advanced(r, field, group, *weight)

    def step_into(r, target):
        for group in range(0, groups, 2):
            weight, next_weight = shares(r, group), shares(r, group + 1)
            for field in range(fields):
                pair = (
                    advanced(r, field, group, *weight),
                    advanced(r, field, group + 1, *next_weight),
                )
                target[pl.ds(field * levels + group * 8, 16)] = jnp.concatenate(
                    pair, axis=0
                ).astype(jnp.bfloat16)

    def transform(source, i):
        partial[i] = jnp.dot(source[...], waves[...], preferred_element_type=jnp.float32)

    def combine(i):
        half_copy(i).wait_recv()
        total = partial[i, own] + half_in[i]
        partial[i, own] = total
        largest = jnp.maximum(jnp.max(jnp.abs(total), axis=1, keepdims=True), 1e-30)
        power = jnp.ceil(jnp.log2(largest))
        code = jnp.round(total * (jnp.exp2(-power) * 32767.0))
        code = jnp.clip(code, -32767.0, 32767.0)
        place = lax.broadcasted_iota(jnp.int32, (half, 2 * KC), 1)
        code = jnp.where(place == KC, power, code)
        coded[i] = code.astype(jnp.int32).astype(jnp.int16)

    wave = lax.rem(lax.broadcasted_iota(jnp.int32, (8, 2 * KC), 1), KC)
    weight = jnp.where(wave == 0, 1.0 / circle_size, 2.0 / circle_size).astype(jnp.float32)

    def finish(i):
        @pl.when(i < RELAYED)
        def _():
            for k in range(2):
                pass_copy(i, k).wait_recv()

        @pl.when(i >= RELAYED)
        def _():
            code_copy(i).wait_recv()

        code = coded_in[i].astype(jnp.int32).astype(jnp.float32)
        unit = jnp.exp2(code[:, KC : KC + 1]) * (1.0 / 32767.0)
        place = lax.broadcasted_iota(jnp.int32, (half, 2 * KC), 1)
        turned_by = jnp.where(lax.rem(place, 2) == 0, 1.0, -1.0)
        code = code * jnp.where(place == KC, 0.0, turned_by)
        total = partial[i, own] + code * unit
        limit = cutoff[lat * rows + row_at(i)]
        scale = jnp.where(wave <= limit, weight, 0.0)
        scaled = total.reshape(half // 8, 8, 2 * KC) * scale[None]
        spectra[i, own] = scaled.reshape(half, 2 * KC).astype(jnp.bfloat16)
        join_copy(i).start()

    def merge(i):
        join_copy(i).wait_recv()
        r = row_at(i)
        smooth = jnp.dot(spectra[i], turned[...], preferred_element_type=jnp.float32)
        smooth = smooth.astype(jnp.bfloat16).astype(jnp.float32)
        smooth = smooth.reshape(fields, levels, columns)
        kept = jnp.full((8, columns), mask[lat * rows + r], jnp.int32) != 0
        for field in range(fields):
            for group in range(groups):
                span = pl.ds(group * 8, 8)
                results[r, field, span] = jnp.where(
                    kept, smooth[field, group * 8 : group * 8 + 8], results[r, field, span]
                )

    def send_code(i):
        @pl.when(i < RELAYED)
        def _():
            for k in range(2):
                lend_copy(i, k).start()

        @pl.when(i >= RELAYED)
        def _():
            code_copy(i).start()

    def combine_and_send(i):
        combine(i)
        send_code(i)

    pairs = (rows - 2) // 2

    @pl.when(polar)
    def _():
        table_copies()[0].wait()
        odd_lines[...] = jnp.zeros_like(odd_lines)

        def two_rows(j, carry):
            i = 2 * j
            ready(i + 1)
            transform(odd_lines, jnp.where(j == 0, rows, i - 1))
            step_into(i + 1, even_lines)

            @pl.when(j >= 1)
            def _():
                half_copy(i - 1).start()

            @pl.when(j >= 2)
            def _():
                combine_and_send(i - 4)

            ready(i + 2)
            transform(even_lines, i)
            step_into(i + 2, odd_lines)
            half_copy(i).start()

            @pl.when(j >= 2)
            def _():
                combine_and_send(i - 3)

            return carry

        lax.fori_loop(0, pairs, two_rows, 0)
        transform(odd_lines, rows - 3)
        half_copy(rows - 3).start()
        combine_and_send(rows - 6)
        combine_and_send(rows - 5)
        combine_and_send(rows - 4)
        combine_and_send(rows - 3)
        turn_back()

    @pl.when(jnp.logical_not(polar))
    def _():
        def one_row(r, carry):
            ready(r)
            step(r)
            return carry

        lax.fori_loop(1, rows - 1, one_row, 0)

    @pl.when(middle)
    def _():
        for p in range(RELAYED):
            for k in range(2):
                lend_copy(p, k).wait_recv()
                pass_copy(p, k).start()

    ready(0)
    ready(rows - 1)
    for field in range(fields):
        for side, r in ((1, rows - 1), (0, 0)):
            edge_copy(0, field, side, (lat, across)).wait_recv()
            xs[side * (rows + 1), field] = halos[side, field].astype(jnp.float32)
            for group in range(groups):
                advanced(r, field, group, *shares(r, group))

    @pl.when(polar)
    def _():
        for i, lines_of in ((rows - 2, even_lines), (rows - 1, odd_lines)):
            r = row_at(i)
            lines_of[...] = results[r].reshape(lines, columns).astype(jnp.bfloat16)
            transform(lines_of, i)
            half_copy(i).start()
        def position(t):
            return jnp.where(t < 2 * RELAYED, t // 2 + RELAYED * (1 - lax.rem(t, 2)), t)

        finish(position(0))
        finish(position(1))
        combine_and_send(rows - 2)
        combine_and_send(rows - 1)

        def endings(t, carry):
            merge(position(t - 2))
            finish(position(t))
            return carry

        lax.fori_loop(2, rows - 1, endings, 0)
        merge(position(rows - 3))
        merge(position(rows - 2))
        finish(rows - 1)
        merge(rows - 1)

        def drain(i, carry):
            half_copy(i).wait_send()
            join_copy(i).wait_send()

            @pl.when(i < RELAYED)
            def _():
                for k in range(2):
                    lend_copy(i, k).wait_send()

            @pl.when(i >= RELAYED)
            def _():
                code_copy(i).wait_send()

            return carry

        lax.fori_loop(0, rows, drain, 0)

    @pl.when(middle)
    def _():
        for p in range(RELAYED):
            for k in range(2):
                pass_copy(p, k).wait_send()

    for k in range(2):
        remote(
            edges.at[k], halos.at[k], edge_send.at[k], edge_recv.at[k, 0], (lat, across)
        ).wait_send()
        remote(
            columns_out.at[k],
            columns_in.at[k],
            column_send.at[k],
            column_recv.at[k, 0],
            (lat, after),
        ).wait_send()


def place_kernel(stepped, out, sem):
    copies = [
        pltpu.make_async_copy(stepped.at[r], out.at[:, :, r], sem.at[r])
        for r in range(stepped.shape[0])
    ]
    for copy in copies:
        copy.start()
    for copy in copies:
        copy.wait()


def with_caps(state_fields, stencil_weights, filter_mask, cutoff_wave):
    fields, levels, rows, columns = state_fields.shape
    lon_count = lax.axis_size("lon")
    lines = fields * levels
    half = lines // 2
    whole_table = roots_table(2 * columns, columns * lon_count)
    table = whole_table[:columns]
    dma = pltpu.SemaphoreType.DMA
    in_hbm = pl.BlockSpec(memory_space=pl.ANY)
    in_vmem = pl.BlockSpec(memory_space=pltpu.VMEM)
    f32, bf16, i16 = jnp.float32, jnp.bfloat16, jnp.int16
    stepped = pl.pallas_call(
        caps_kernel,
        in_specs=[in_hbm] * 6,
        out_specs=in_vmem,
        out_shape=jax.ShapeDtypeStruct((rows, fields, levels, columns), f32),
        scratch_shapes=[
            pltpu.VMEM((rows + 2, fields, levels, columns), f32),
            pltpu.VMEM((rows, 4, levels, columns), f32),
            pltpu.VMEM((columns, 2 * KC), bf16),
            pltpu.VMEM((2 * KC, columns), bf16),
            pltpu.SMEM(filter_mask.shape, jnp.int32),
            pltpu.SMEM(cutoff_wave.shape, jnp.int32),
            pltpu.VMEM((lines, columns), bf16),
            pltpu.VMEM((lines, columns), bf16),
            pltpu.VMEM((2, fields, levels, columns), bf16),
            pltpu.VMEM((2, fields, levels, columns), bf16),
            pltpu.VMEM((2, rows, 8, 128), f32),
            pltpu.VMEM((2, rows, 8, 128), f32),
            pltpu.VMEM((rows + 1, lines, 2 * KC), f32),
            pltpu.VMEM((rows, half, 2 * KC), f32),
            pltpu.VMEM((rows, half, 2 * KC), i16),
            pltpu.VMEM((rows, half, 2 * KC), i16),
            pltpu.VMEM((RELAYED, half, 2 * KC), i16),
            pltpu.VMEM((rows, lines, 2 * KC), bf16),
            dma((rows,)),
            dma((rows,)),
            dma((4,)),
            dma((2,)),
            dma((2, fields)),
            dma((2,)),
            dma((2, rows)),
            dma((rows,)),
            dma((rows,)),
            dma((rows,)),
            dma((rows,)),
            dma((RELAYED, 2)),
            dma((RELAYED, 2)),
            dma((RELAYED, 2)),
            dma((RELAYED, 2)),
            dma((rows,)),
            dma((rows,)),
        ],
        compiler_params=pltpu.CompilerParams(
            collective_id=1, has_side_effects=True, vmem_limit_bytes=40_000_000
        ),
        name="caps",
    )(
        *(
            pltpu.with_memory_space_constraint(array, pltpu.HBM)
            for array in (
                state_fields,
                stencil_weights,
                filter_mask,
                cutoff_wave,
                jnp.asarray(whole_table.reshape(2, columns, 2 * KC)),
                jnp.asarray(np.ascontiguousarray(table.T)),
            )
        )
    )
    return pl.pallas_call(
        place_kernel,
        in_specs=[in_vmem],
        out_specs=in_hbm,
        out_shape=jax.ShapeDtypeStruct(state_fields.shape, f32),
        scratch_shapes=[dma((rows,))],
        compiler_params=pltpu.CompilerParams(vmem_limit_bytes=1 << 20),
        name="place",
    )(stepped)


def cap_rows(lat_rows):
    return {64: 8, 256: 40}.get(lat_rows, lat_rows)


def solution(mesh):
    def body(state_fields, stencil_weights, filter_mask, cutoff_wave):
        fields, levels, rows, columns = state_fields.shape
        one_block = cap_rows(filter_mask.shape[0]) <= rows
        suits = rows == 8 and columns % 128 == 0 and fields * levels % 32 == 0 and levels % 16 == 0
        if one_block and suits and mesh.shape["lon"] == 4 and mesh.shape["lat"] >= 6:
            return with_caps(state_fields, stencil_weights, filter_mask, cutoff_wave)
        return on_device(state_fields, stencil_weights, filter_mask, cutoff_wave)

    return jax.shard_map(
        body,
        mesh=mesh,
        in_specs=(P(None, None, "lat", "lon"), P(None, None, "lat", "lon"), P(), P()),
        out_specs=P(None, None, "lat", "lon"),
        check_vma=False,
    )
```

```python
import math

import jax
import jax.numpy as jnp
import numpy as np
from jax import lax
from jax.experimental import pallas as pl
from jax.experimental.pallas import tpu as pltpu
from jax.sharding import PartitionSpec as P

KC = 256


def angle_parts(columns, circle_size, axis):
    waves = lax.broadcasted_iota(
        jnp.int32, (columns.size, KC) if axis == 1 else (KC, columns.size), axis
    )
    product = jnp.expand_dims(columns, axis) * waves % circle_size
    angles = product.astype(jnp.float32) * (2.0 * math.pi / circle_size)
    return jnp.cos(angles), jnp.sin(angles)


MESH = pl.DeviceIdType.MESH


def step_kernel(
    state,
    weights,
    cosines,
    sines,
    turned_cosines,
    turned_sines,
    bounds,
    results,
    waves,
    turned,
    rounded,
    top,
    bottom,
    north,
    south,
    columns_out,
    columns_in,
    sides,
    partial,
    halves,
    quarters,
    half_in,
    quarter_in,
    spectra,
    row_send,
    row_recv,
    side_send,
    side_recv,
    sum_send,
    sum_recv,
    join_send,
    join_recv,
):
    fields, lines, columns = state.shape
    chunks, _, size, _ = top.shape
    depth = lines // chunks
    rows = depth // size
    modes = waves.shape[1] // 2
    half = partial.shape[1] // 2
    quarter = half // 2
    lat_count, lon_count = lax.axis_size("lat"), lax.axis_size("lon")
    lat, lon = lax.axis_index("lat"), lax.axis_index("lon")
    after = lax.rem(lon + 1, lon_count)
    before = lax.rem(lon + lon_count - 1, lon_count)
    across = lax.rem(lon + lon_count // 2, lon_count)
    bits = lon_count.bit_length() - 1
    digit = [lax.rem(lon // (1 << b), 2) for b in range(bits)]
    peer = [lon + (1 << b) - (2 << b) * digit[b] for b in range(bits)]
    own_half = digit[0] * half
    own_quarter = digit[1] * quarter

    def span_of(g, first, count):
        return pl.ds(pl.multiple_of(g * depth + first, count), count)

    def remote(source, target, sent, got, device):
        return pltpu.make_async_remote_copy(
            src_ref=source,
            dst_ref=target,
            send_sem=sent,
            recv_sem=got,
            device_id=device,
            device_id_type=MESH,
        )

    def row_copy(g, up, device, into_north):
        return remote(
            top.at[g] if up else bottom.at[g],
            north.at[g] if into_north else south.at[g],
            row_send.at[0 if up else 1, g],
            row_recv.at[0 if into_north else 1, g],
            device,
        )

    def side_copy(k, device):
        return remote(
            columns_out.at[k], columns_in.at[k], side_send.at[k], side_recv.at[k], device
        )

    def sum_copy(b, g):
        if b == 0:
            away = pl.ds(pl.multiple_of((1 - digit[0]) * half, 16), half)
            source, target = partial.at[g, away], half_in.at[g]
        elif b == 1:
            away = pl.ds(pl.multiple_of((1 - digit[1]) * quarter, 16), quarter)
            source, target = halves.at[g, away], quarter_in.at[0, g]
        else:
            source, target = quarters.at[b - 2, g], quarter_in.at[b - 1, g]
        return remote(source, target, sum_send.at[b, g], sum_recv.at[b, g], (lat, peer[b]))

    def join_copy(b, g):
        if b == 0:
            part = pl.ds(pl.multiple_of(own_half, 16), half)
        else:
            part = pl.ds(pl.multiple_of(own_half + own_quarter, 16), quarter)
        view = spectra.at[g, part]
        return remote(view, view, join_send.at[b, g], join_recv.at[b, g], (lat, peer[b]))

    barrier = pltpu.get_barrier_semaphore()
    for other in (after, before, across, *peer):
        pl.semaphore_signal(barrier, inc=1, device_id=(lat, other), device_id_type=MESH)

    @pl.when(lat > 0)
    def _():
        pl.semaphore_signal(barrier, inc=1, device_id=(lat - 1, lon), device_id_type=MESH)

    @pl.when(lat < lat_count - 1)
    def _():
        pl.semaphore_signal(barrier, inc=1, device_id=(lat + 1, lon), device_id_type=MESH)

    inside = (lat > 0) & (lat < lat_count - 1)

    @pl.when(inside)
    def _():
        pl.semaphore_wait(barrier, 5 + bits)

    @pl.when(jnp.logical_not(inside))
    def _():
        pl.semaphore_wait(barrier, 4 + bits)

    taker = lax.broadcasted_iota(jnp.int32, (2 * size, depth), 0)
    taken = lax.broadcasted_iota(jnp.int32, (2 * size, depth), 1)
    wanted = jnp.where(taker < size, taker * rows, (taker - size) * rows + rows - 1)
    gather = jnp.where(taken == wanted, 1.0, 0.0).astype(jnp.bfloat16)

    def send_rows(g, carry):
        for field in range(fields):
            sign = -1.0 if field < 2 else 1.0
            up_sign = jnp.where(lat == 0, sign, 1.0).astype(jnp.float32)
            down_sign = jnp.where(lat == lat_count - 1, sign, 1.0).astype(jnp.float32)
            edges = jnp.dot(
                gather,
                state[field, span_of(g, 0, depth)].astype(jnp.bfloat16),
                preferred_element_type=jnp.float32,
            )
            top[g, field] = (edges[:size] * up_sign).astype(jnp.bfloat16)
            bottom[g, field] = (edges[size:] * down_sign).astype(jnp.bfloat16)

        @pl.when(lat == 0)
        def _():
            row_copy(g, True, (lat, across), True).start()

        @pl.when(lat > 0)
        def _():
            row_copy(g, True, (lat - 1, lon), False).start()

        @pl.when(lat < lat_count - 1)
        def _():
            row_copy(g, False, (lat + 1, lon), True).start()

        @pl.when(lat == lat_count - 1)
        def _():
            row_copy(g, False, (lat, across), False).start()

        return carry

    lax.fori_loop(0, chunks, send_rows, 0)

    spot = lax.broadcasted_iota(jnp.int32, (16, 128), 1)
    line = lax.broadcasted_iota(jnp.int32, (16, 128), 0)

    def pick(k, lanes, lane):
        chosen = jnp.where((spot == lane) & (line == 0), 1.0, 0.0).astype(jnp.bfloat16)
        for g in range(chunks):
            for field in range(0, fields):
                first = (g * fields + field) * depth
                edge = state[field, span_of(g, 0, depth), lanes].astype(jnp.bfloat16)
                picked = lax.dot_general(
                    chosen, edge, (((1,), (1,)), ((), ())), preferred_element_type=jnp.float32
                )
                columns_out[k, g * fields + field] = picked.astype(jnp.bfloat16)

    pick(0, pl.ds(columns - 128, 128), 127)
    side_copy(0, (lat, after)).start()
    pick(1, pl.ds(0, 128), 0)
    side_copy(1, (lat, before)).start()

    fine = 32
    coarse = columns // fine
    fine_cos, fine_sin = cosines[coarse:], sines[coarse:]

    def fill(at, carry):
        span = pl.ds(pl.multiple_of(at * fine, fine), fine)
        coarse_cos, coarse_sin = cosines[pl.ds(at, 1)], sines[pl.ds(at, 1)]
        waves[span, :modes] = (coarse_cos * fine_cos - coarse_sin * fine_sin).astype(jnp.bfloat16)
        waves[span, modes:] = (coarse_sin * fine_cos + coarse_cos * fine_sin).astype(jnp.bfloat16)
        return carry

    lax.fori_loop(0, coarse, fill, 0)
    lane_cos, lane_sin = turned_cosines[:, :128], turned_sines[:, :128]
    for at in range(columns // 128):
        span = pl.ds(at * 128, 128)
        tile_cos = turned_cosines[:, 128 + at : 129 + at]
        tile_sin = turned_sines[:, 128 + at : 129 + at]
        turned[:modes, span] = (tile_cos * lane_cos - tile_sin * lane_sin).astype(jnp.bfloat16)
        turned[modes:, span] = (tile_sin * lane_cos + tile_cos * lane_sin).astype(jnp.bfloat16)

    spread = jnp.where(line == 0, 1.0, 0.0).astype(jnp.bfloat16)
    for k in range(2):
        side_copy(k, (lat, after)).wait_recv()
        for at in range(chunks * fields):
            sides[k, at] = lax.dot_general(
                columns_in[k, at],
                spread,
                (((0,), (0,)), ((), ())),
                preferred_element_type=jnp.float32,
            )

    lane = lax.broadcasted_iota(jnp.int32, (rows, columns), 1)
    level_line = lax.broadcasted_iota(jnp.int32, (rows, columns), 0)
    copies = columns // 128

    wave = lax.rem(lax.broadcasted_iota(jnp.int32, (rows, 2 * modes), 1), modes)
    circle_size = columns * lon_count
    weight = jnp.where(wave == 0, 1.0 / circle_size, 2.0 / circle_size)
    scale = jnp.where(wave <= bounds[:, 1:2], weight, 0.0).astype(jnp.float32)

    def advance(g):
        row_copy(g, True, (lat, across), True).wait_recv()
        row_copy(g, False, (lat, across), False).wait_recv()

        def one_field(field, inner):
            above = north[g, field].astype(jnp.float32)
            below = south[g, field].astype(jnp.float32)
            for level in range(0, size, 2):
                pair = []
                for at in (level, level + 1):
                    span = pl.ds(at * rows, rows)
                    here = span_of(g, at * rows, rows)
                    x = state[field, here]
                    left = jnp.concatenate([sides[0, g * fields + field, span]] * copies, axis=1)
                    right = jnp.concatenate([sides[1, g * fields + field, span]] * copies, axis=1)
                    w = jnp.where(lane == 0, left, pltpu.roll(x, 1, 1))
                    e = jnp.where(lane == columns - 1, right, pltpu.roll(x, columns - 1, 1))
                    n = jnp.where(level_line == 0, above[at : at + 1], pltpu.roll(x, 1, 0))
                    s = jnp.where(
                        level_line == rows - 1, below[at : at + 1], pltpu.roll(x, rows - 1, 0)
                    )
                    y = (
                        x
                        + weights[0, here] * (e - x)
                        + weights[1, here] * (w - x)
                        + weights[2, here] * (n - x)
                        + weights[3, here] * (s - x)
                    )
                    results[field, here] = y
                    pair.append(y)
                first = pl.multiple_of(field * depth + level * rows, 2 * rows)
                rounded[pl.ds(first, 2 * rows), :] = jnp.concatenate(pair, axis=0).astype(
                    jnp.bfloat16
                )
            return inner

        lax.fori_loop(0, fields, one_field, 0)
        partial[g] = jnp.dot(rounded[...], waves[...], preferred_element_type=jnp.float32)
        sum_copy(0, g).start()

    def pair_sum(g):
        sum_copy(0, g).wait_recv()
        mine = pl.ds(pl.multiple_of(own_half, 16), half)
        halves[g] = partial[g, mine] + half_in[g]
        sum_copy(1, g).start()

    def full_sum(g):
        sum_copy(1, g).wait_recv()
        mine = pl.ds(pl.multiple_of(own_quarter, 16), quarter)
        total = halves[g, mine] + quarter_in[0, g]
        for b in range(2, bits):
            quarters[b - 2, g] = total
            sum_copy(b, g).start()
            sum_copy(b, g).wait_recv()
            total = total + quarter_in[b - 1, g]
        scaled = total.reshape(quarter // rows, rows, 2 * modes) * scale[None]
        part = pl.ds(pl.multiple_of(own_half + own_quarter, 16), quarter)
        spectra[g, part] = scaled.reshape(quarter, 2 * modes).astype(jnp.bfloat16)
        join_copy(1, g).start()

    def join(g):
        join_copy(1, g).wait_recv()
        join_copy(0, g).start()

    def merge(g):
        join_copy(0, g).wait_recv()
        smooth = jnp.dot(spectra[g], turned[...], preferred_element_type=jnp.float32)
        smooth = smooth.astype(jnp.bfloat16).astype(jnp.float32)
        smooth = smooth.reshape(fields, size, rows, columns)
        kept = jnp.broadcast_to(bounds[:, 0:1], (rows, columns)) != 0
        for field in range(fields):
            for at in range(size):
                here = span_of(g, at * rows, rows)
                results[field, here] = jnp.where(kept, smooth[field, at], results[field, here])

    def forward(t, carry):
        advance(t)

        @pl.when(t >= 1)
        def _():
            pair_sum(t - 1)

        return carry

    last = chunks - 1
    lax.fori_loop(0, chunks, forward, 0)
    full_sum(0)
    pair_sum(last)

    def sums(g, carry):
        full_sum(g)
        return carry

    def joins(g, carry):
        join(g)
        return carry

    def merges(g, carry):
        merge(g)

        @pl.when(g + 2 < chunks)
        def _():
            join(g + 2)

        return carry

    lax.fori_loop(1, last, sums, 0)
    lax.fori_loop(0, 2, joins, 0)
    full_sum(last)
    lax.fori_loop(0, chunks, merges, 0)

    def finish(g, carry):
        for b in range(bits):
            sum_copy(b, g).wait_send()
        for b in range(2):
            join_copy(b, g).wait_send()
        row_copy(g, True, (lat, across), True).wait_send()
        row_copy(g, False, (lat, across), False).wait_send()
        return carry

    lax.fori_loop(0, chunks, finish, 0)
    for k in range(2):
        side_copy(k, (lat, after)).wait_send()


def on_device(state_fields, stencil_weights, filter_mask, cutoff_wave):
    fields, levels, rows, columns = state_fields.shape
    lat_count, lon_count = lax.axis_size("lat"), lax.axis_size("lon")
    lat_pos, lon_pos = lax.axis_index("lat"), lax.axis_index("lon")
    circle_size = columns * lon_count
    size = 8
    steps = levels // size
    start = lat_pos * rows
    bounds = lax.dynamic_slice_in_dim(jnp.stack([filter_mask, cutoff_wave], axis=1), start, rows)
    origin = lon_pos * columns
    cosines, sines = angle_parts(
        jnp.concatenate(
            [origin + 32 * jnp.arange(columns // 32), jnp.arange(32)]
        ).astype(jnp.int32),
        circle_size,
        1,
    )
    turned_cosines, turned_sines = angle_parts(
        jnp.concatenate(
            [jnp.arange(128), origin + 128 * jnp.arange(columns // 128)]
        ).astype(jnp.int32),
        circle_size,
        0,
    )
    rows_each = fields * size * rows
    depth = size * rows
    dma = pltpu.SemaphoreType.DMA
    strip = pltpu.VMEM((steps, fields, size, columns), jnp.bfloat16)
    column_strip = pltpu.VMEM((2, steps * fields, 16, depth), jnp.bfloat16)
    extra = max(lon_count.bit_length() - 3, 1)
    in_vmem = pl.BlockSpec(memory_space=pltpu.VMEM)
    bits = lon_count.bit_length() - 1
    advanced = pl.pallas_call(
        step_kernel,
        in_specs=[in_vmem] * 7,
        out_specs=in_vmem,
        out_shape=jax.ShapeDtypeStruct((fields, levels * rows, columns), jnp.float32),
        scratch_shapes=[
            pltpu.VMEM((columns, 2 * KC), jnp.bfloat16),
            pltpu.VMEM((2 * KC, columns), jnp.bfloat16),
            pltpu.VMEM((rows_each, columns), jnp.bfloat16),
            strip,
            strip,
            strip,
            strip,
            column_strip,
            column_strip,
            pltpu.VMEM((2, steps * fields, depth, 128), jnp.float32),
            pltpu.VMEM((steps, rows_each, 2 * KC), jnp.float32),
            pltpu.VMEM((steps, rows_each // 2, 2 * KC), jnp.float32),
            pltpu.VMEM((extra, steps, rows_each // 4, 2 * KC), jnp.float32),
            pltpu.VMEM((steps, rows_each // 2, 2 * KC), jnp.float32),
            pltpu.VMEM((bits - 1, steps, rows_each // 4, 2 * KC), jnp.float32),
            pltpu.VMEM((steps, rows_each, 2 * KC), jnp.bfloat16),
            dma((2, steps)),
            dma((2, steps)),
            dma((2,)),
            dma((2,)),
            dma((bits, steps)),
            dma((bits, steps)),
            dma((2, steps)),
            dma((2, steps)),
        ],
        compiler_params=pltpu.CompilerParams(
            collective_id=0, has_side_effects=True, vmem_limit_bytes=38 << 20
        ),
        name="step",
    )(
        state_fields.reshape(fields, levels * rows, columns),
        stencil_weights.reshape(4, levels * rows, columns),
        cosines,
        sines,
        turned_cosines,
        turned_sines,
        bounds,
    )
    return advanced.reshape(state_fields.shape)


def roots_table(columns, circle_size):
    steps = np.arange(columns)[:, None] * np.arange(KC)[None, :] % circle_size
    angles = steps * (2.0 * np.pi / circle_size)
    return np.concatenate([np.cos(angles), np.sin(angles)], axis=1).astype(jnp.bfloat16)


def quarter_turns(shape, axis, turns):
    phase = lax.rem(lax.broadcasted_iota(jnp.int32, shape, axis) * turns, 4)
    a = jnp.where(phase == 0, 1.0, jnp.where(phase == 2, -1.0, 0.0))
    b = jnp.where(phase == 1, 1.0, jnp.where(phase == 3, -1.0, 0.0))
    return a.astype(jnp.bfloat16), b.astype(jnp.bfloat16)


RELAYED = 3


def caps_kernel(
    state,
    weights,
    mask_in,
    cutoff_in,
    waves_in,
    turned_in,
    results,
    xs,
    ws,
    waves,
    turned,
    mask,
    cutoff,
    even_lines,
    odd_lines,
    edges,
    halos,
    columns_out,
    columns_in,
    partial,
    half_in,
    coded,
    coded_in,
    passing,
    spectra,
    state_sem,
    weight_sem,
    table_sem,
    edge_send,
    edge_recv,
    column_send,
    column_recv,
    half_send,
    half_recv,
    code_send,
    code_recv,
    lend_send,
    lend_recv,
    pass_send,
    pass_recv,
    join_send,
    join_recv,
):
    rows, fields, levels, columns = results.shape
    groups = levels // 8
    lines = fields * levels
    half = lines // 2
    lat_count, lon_count = lax.axis_size("lat"), lax.axis_size("lon")
    lat, lon = lax.axis_index("lat"), lax.axis_index("lon")
    after = lax.rem(lon + 1, lon_count)
    before = lax.rem(lon + lon_count - 1, lon_count)
    across = lax.rem(lon + lon_count // 2, lon_count)
    core = lax.rem(lon, 2)
    partner = lon + 1 - 2 * core
    circle_size = columns * lon_count
    first, last = lat == 0, lat == lat_count - 1
    polar = first | last
    middle = (lat == 2) | (lat == lat_count - 3)
    helper = jnp.where(first, 2, lat_count - 3)
    served = jnp.where(lat == 2, 0, lat_count - 1)
    edge_row = jnp.where(last, 0, rows - 1)

    def row_at(i):
        return jnp.where(i < rows - 2, i + 1, jnp.where(i == rows - 2, edge_row, rows - 1 - edge_row))

    own = pl.ds(pl.multiple_of(core * half, 16), half)
    other = pl.ds(pl.multiple_of((1 - core) * half, 16), half)

    def remote(source, target, sent, got, device):
        return pltpu.make_async_remote_copy(
            src_ref=source,
            dst_ref=target,
            send_sem=sent,
            recv_sem=got,
            device_id=device,
            device_id_type=MESH,
        )

    def state_copy(r):
        return pltpu.make_async_copy(state.at[:, :, r], xs.at[r + 1], state_sem.at[r])

    def weight_copy(r):
        return pltpu.make_async_copy(weights.at[:, :, r], ws.at[r], weight_sem.at[r])

    def table_copies():
        return (
            pltpu.make_async_copy(waves_in.at[core], waves, table_sem.at[0]),
            pltpu.make_async_copy(turned_in, turned, table_sem.at[1]),
        )

    def bound_copies():
        return (
            pltpu.make_async_copy(mask_in, mask, table_sem.at[2]),
            pltpu.make_async_copy(cutoff_in, cutoff, table_sem.at[3]),
        )

    def edge_copy(k, field, side, device):
        return remote(
            edges.at[k, field],
            halos.at[side, field],
            edge_send.at[k],
            edge_recv.at[side, field],
            device,
        )

    def column_copy(k, r, device):
        return remote(
            columns_out.at[k, r],
            columns_in.at[k, r],
            column_send.at[k],
            column_recv.at[k, r],
            device,
        )

    def half_copy(i):
        return remote(
            partial.at[i, other], half_in.at[i], half_send.at[i], half_recv.at[i], (lat, partner)
        )

    def code_copy(i):
        return remote(
            coded.at[i], coded_in.at[i], code_send.at[i], code_recv.at[i], (lat, across)
        )

    first_piece = (half // 2 + 15) // 16 * 16
    pieces = (pl.ds(0, first_piece), pl.ds(first_piece, half - first_piece))

    def lend_copy(i, k):
        return remote(
            coded.at[i, pieces[k]],
            passing.at[i, pieces[k]],
            lend_send.at[i, k],
            pass_recv.at[i, k],
            (helper, across),
        )

    def pass_copy(i, k):
        return remote(
            passing.at[i, pieces[k]],
            coded_in.at[i, pieces[k]],
            pass_send.at[i, k],
            lend_recv.at[i, k],
            (served, lon),
        )

    def join_copy(i):
        view = spectra.at[i, own]
        return remote(view, view, join_send.at[i], join_recv.at[i], (lat, partner))

    barrier = pltpu.get_barrier_semaphore()

    def greet(a, b):
        pl.semaphore_signal(barrier, inc=1, device_id=(a, b), device_id_type=MESH)

    for b in (after, before, across):
        greet(lat, b)

    @pl.when(lat > 0)
    def _():
        greet(lat - 1, lon)

    @pl.when(lat < lat_count - 1)
    def _():
        greet(lat + 1, lon)

    @pl.when(polar)
    def _():
        greet(helper, lon)
        greet(helper, across)

    @pl.when(middle)
    def _():
        greet(served, lon)
        greet(served, across)

    for r in (0, rows - 1, *range(1, rows - 1)):
        state_copy(r).start()

    @pl.when(polar)
    def _():
        for copy in table_copies():
            copy.start()

    for copy in bound_copies():
        copy.start()
    for r in (*range(1, rows - 1), 0, rows - 1):
        weight_copy(r).start()

    for r in (0, rows - 1):
        state_copy(r).wait()
    for field in range(fields):
        sign = -1.0 if field < 2 else 1.0
        up_sign = jnp.where(first, sign, 1.0).astype(jnp.float32)
        down_sign = jnp.where(last, sign, 1.0).astype(jnp.float32)
        edges[0, field] = (xs[1, field] * up_sign).astype(jnp.bfloat16)
        edges[1, field] = (xs[rows, field] * down_sign).astype(jnp.bfloat16)

    @pl.when(polar)
    def _():
        pl.semaphore_wait(barrier, 3 + 1 + 2)

    @pl.when(middle)
    def _():
        pl.semaphore_wait(barrier, 3 + 2 + 2)

    @pl.when(jnp.logical_not(polar | middle))
    def _():
        pl.semaphore_wait(barrier, 3 + 2)

    def send_up(field):
        @pl.when(lat > 0)
        def _():
            edge_copy(0, field, 1, (lat - 1, lon)).start()

    def send_down(field):
        @pl.when(lat < lat_count - 1)
        def _():
            edge_copy(1, field, 0, (lat + 1, lon)).start()

    beside_first, beside_last = lat == 1, lat == lat_count - 2

    @pl.when(beside_first)
    def _():
        for field in range(fields):
            send_up(field)
        for field in range(fields):
            send_down(field)

    @pl.when(beside_last)
    def _():
        for field in range(fields):
            send_down(field)
        for field in range(fields):
            send_up(field)

    @pl.when(jnp.logical_not(beside_first | beside_last))
    def _():
        for field in range(fields):
            send_up(field)
            send_down(field)

    spot = lax.broadcasted_iota(jnp.int32, (8, 128), 1)

    def send_columns(r):
        to_after = jnp.zeros((8, 128), jnp.float32)
        to_before = jnp.zeros((8, 128), jnp.float32)
        for group in range(groups):
            for field in range(fields):
                at = group * fields + field
                span = pl.ds(group * 8, 8)
                right = xs[r + 1, field, span, pl.ds(columns - 128, 128)]
                left = xs[r + 1, field, span, pl.ds(0, 128)]
                to_after = jnp.where(spot == at, pltpu.roll(right, at + 1, 1), to_after)
                left = pltpu.roll(left, at, 1) if at else left
                to_before = jnp.where(spot == at, left, to_before)
        columns_out[0, r] = to_after
        columns_out[1, r] = to_before
        column_copy(0, r, (lat, after)).start()
        column_copy(1, r, (lat, before)).start()

    def send_rim(field):
        @pl.when(first)
        def _():
            edge_copy(0, field, 0, (lat, across)).start()

        @pl.when(last)
        def _():
            edge_copy(1, field, 1, (lat, across)).start()

    for r in (*range(1, rows - 1), rows - 1, 0):
        if 0 < r < rows - 1:
            state_copy(r).wait()
        send_columns(r)
        if r == 3:
            send_rim(0)
    for field in range(1, fields):
        send_rim(field)

    for copy in bound_copies():
        copy.wait()

    def turn_back():
        table_copies()[1].wait()
        a, b = quarter_turns((16, 128), 0, core)

        def turn(t, carry):
            low = pl.ds(pl.multiple_of(t * 16, 16), 16)
            high = pl.ds(pl.multiple_of(KC + t * 16, 16), 16)
            for tile in range(columns // 128):
                lanes = pl.ds(tile * 128, 128)
                c, s = turned[low, lanes], turned[high, lanes]
                turned[low, lanes] = a * c - b * s
                turned[high, lanes] = a * s + b * c
            return carry

        lax.fori_loop(0, KC // 16, turn, 0)

    tiles = columns // 128

    def shares(r, group):
        span = pl.ds(group * 8, 8)
        return [ws[r, q, span] for q in range(4)]

    def advanced(r, field, group, east_w, west_w, north_w, south_w):
        at = group * fields + field
        span = pl.ds(group * 8, 8)
        x = xs[r + 1, field, span]
        n = xs[r, field, span]
        s = xs[r + 2, field, span]
        parts = [x[:, t * 128 : t * 128 + 128] for t in range(tiles)]
        left = columns_in[0, r]
        left = pltpu.roll(left, 128 - at, 1) if at else left
        right = pltpu.roll(columns_in[1, r], 127 - at, 1)
        to_right = [left] + [pltpu.roll(p, 1, 1) for p in parts]
        to_left = [pltpu.roll(p, 127, 1) for p in parts] + [right]
        w = [jnp.where(spot == 0, to_right[t], to_right[t + 1]) for t in range(tiles)]
        e = [jnp.where(spot == 127, to_left[t + 1], to_left[t]) for t in range(tiles)]
        y = (
            x
            + east_w * (jnp.concatenate(e, axis=1) - x)
            + west_w * (jnp.concatenate(w, axis=1) - x)
            + north_w * (n - x)
            + south_w * (s - x)
        )
        results[r, field, span] = y
        return y

    def ready(r):
        column_copy(0, r, (lat, after)).wait_recv()
        column_copy(1, r, (lat, before)).wait_recv()
        weight_copy(r).wait()

    def step(r):
        for group in range(groups):
            weight = shares(r, group)
            for field in range(fields):
                advanced(r, field, group, *weight)

    def step_into(r, target):
        for group in range(0, groups, 2):
            weight, next_weight = shares(r, group), shares(r, group + 1)
            for field in range(fields):
                pair = (
                    advanced(r, field, group, *weight),
                    advanced(r, field, group + 1, *next_weight),
                )
                target[pl.ds(field * levels + group * 8, 16)] = jnp.concatenate(
                    pair, axis=0
                ).astype(jnp.bfloat16)

    def transform(source, i):
        partial[i] = jnp.dot(source[...], waves[...], preferred_element_type=jnp.float32)

    def combine(i):
        half_copy(i).wait_recv()
        total = partial[i, own] + half_in[i]
        partial[i, own] = total
        largest = jnp.maximum(jnp.max(jnp.abs(total), axis=1, keepdims=True), 1e-30)
        power = jnp.ceil(jnp.log2(largest))
        code = jnp.round(total * (jnp.exp2(-power) * 32767.0))
        code = jnp.clip(code, -32767.0, 32767.0)
        place = lax.broadcasted_iota(jnp.int32, (half, 2 * KC), 1)
        code = jnp.where(place == KC, power, code)
        coded[i] = code.astype(jnp.int32).astype(jnp.int16)

    wave = lax.rem(lax.broadcasted_iota(jnp.int32, (8, 2 * KC), 1), KC)
    weight = jnp.where(wave == 0, 1.0 / circle_size, 2.0 / circle_size).astype(jnp.float32)

    def finish(i):
        @pl.when(i < RELAYED)
        def _():
            for k in range(2):
                pass_copy(i, k).wait_recv()

        @pl.when(i >= RELAYED)
        def _():
            code_copy(i).wait_recv()

        code = coded_in[i].astype(jnp.int32).astype(jnp.float32)
        unit = jnp.exp2(code[:, KC : KC + 1]) * (1.0 / 32767.0)
        place = lax.broadcasted_iota(jnp.int32, (half, 2 * KC), 1)
        turned_by = jnp.where(lax.rem(place, 2) == 0, 1.0, -1.0)
        code = code * jnp.where(place == KC, 0.0, turned_by)
        total = partial[i, own] + code * unit
        limit = cutoff[lat * rows + row_at(i)]
        scale = jnp.where(wave <= limit, weight, 0.0)
        scaled = total.reshape(half // 8, 8, 2 * KC) * scale[None]
        spectra[i, own] = scaled.reshape(half, 2 * KC).astype(jnp.bfloat16)
        join_copy(i).start()

    def merge(i):
        join_copy(i).wait_recv()
        r = row_at(i)
        smooth = jnp.dot(spectra[i], turned[...], preferred_element_type=jnp.float32)
        smooth = smooth.astype(jnp.bfloat16).astype(jnp.float32)
        smooth = smooth.reshape(fields, levels, columns)
        kept = jnp.full((8, columns), mask[lat * rows + r], jnp.int32) != 0
        for field in range(fields):
            for group in range(groups):
                span = pl.ds(group * 8, 8)
                results[r, field, span] = jnp.where(
                    kept, smooth[field, group * 8 : group * 8 + 8], results[r, field, span]
                )

    def send_code(i):
        @pl.when(i < RELAYED)
        def _():
            for k in range(2):
                lend_copy(i, k).start()

        @pl.when(i >= RELAYED)
        def _():
            code_copy(i).start()

    def combine_and_send(i):
        combine(i)
        send_code(i)

    pairs = (rows - 2) // 2

    @pl.when(polar)
    def _():
        table_copies()[0].wait()
        turn_back()
        odd_lines[...] = jnp.zeros_like(odd_lines)

        def two_rows(j, carry):
            i = 2 * j
            ready(i + 1)
            transform(odd_lines, jnp.where(j == 0, rows, i - 1))
            step_into(i + 1, even_lines)

            @pl.when(j >= 1)
            def _():
                half_copy(i - 1).start()

            @pl.when(j >= 2)
            def _():
                combine_and_send(i - 4)

            ready(i + 2)
            transform(even_lines, i)
            step_into(i + 2, odd_lines)
            half_copy(i).start()

            @pl.when(j >= 2)
            def _():
                combine_and_send(i - 3)

            return carry

        lax.fori_loop(0, pairs, two_rows, 0)
        transform(odd_lines, rows - 3)
        half_copy(rows - 3).start()
        combine_and_send(rows - 6)
        combine_and_send(rows - 5)
        combine_and_send(rows - 4)
        combine_and_send(rows - 3)

    @pl.when(jnp.logical_not(polar))
    def _():
        def one_row(r, carry):
            ready(r)
            step(r)
            return carry

        lax.fori_loop(1, rows - 1, one_row, 0)

    @pl.when(middle)
    def _():
        for p in range(RELAYED):
            for k in range(2):
                lend_copy(p, k).wait_recv()
                pass_copy(p, k).start()

    def edge_step(i, carry):
        r = row_at(i)
        side = jnp.where(r == 0, 0, 1)
        ready(r)
        for field in range(fields):
            edge_copy(0, field, side, (lat, across)).wait_recv()
            xs[side * (rows + 1), field] = halos[side, field].astype(jnp.float32)
            for group in range(groups):
                advanced(r, field, group, *shares(r, group))

        @pl.when(polar)
        def _():
            even_lines[...] = results[r].reshape(lines, columns).astype(jnp.bfloat16)
            transform(even_lines, i)
            half_copy(i).start()

        return carry

    lax.fori_loop(rows - 2, rows, edge_step, 0)

    @pl.when(polar)
    def _():
        def position(t):
            return jnp.where(t < 2 * RELAYED, t // 2 + RELAYED * (1 - lax.rem(t, 2)), t)

        combine_and_send(rows - 2)
        combine_and_send(rows - 1)
        finish(position(0))
        finish(position(1))

        def endings(t, carry):
            merge(position(t - 2))
            finish(position(t))
            return carry

        lax.fori_loop(2, rows - 1, endings, 0)
        merge(position(rows - 3))
        merge(position(rows - 2))
        finish(rows - 1)
        merge(rows - 1)

        def drain(i, carry):
            half_copy(i).wait_send()
            join_copy(i).wait_send()

            @pl.when(i < RELAYED)
            def _():
                for k in range(2):
                    lend_copy(i, k).wait_send()

            @pl.when(i >= RELAYED)
            def _():
                code_copy(i).wait_send()

            return carry

        lax.fori_loop(0, rows, drain, 0)

    @pl.when(middle)
    def _():
        for p in range(RELAYED):
            for k in range(2):
                pass_copy(p, k).wait_send()

    for k in range(2):
        remote(
            edges.at[k], halos.at[k], edge_send.at[k], edge_recv.at[k, 0], (lat, across)
        ).wait_send()
        remote(
            columns_out.at[k],
            columns_in.at[k],
            column_send.at[k],
            column_recv.at[k, 0],
            (lat, after),
        ).wait_send()


def place_kernel(stepped, out, sem):
    copies = [
        pltpu.make_async_copy(stepped.at[r], out.at[:, :, r], sem.at[r])
        for r in range(stepped.shape[0])
    ]
    for copy in copies:
        copy.start()
    for copy in copies:
        copy.wait()


def with_caps(state_fields, stencil_weights, filter_mask, cutoff_wave):
    fields, levels, rows, columns = state_fields.shape
    lon_count = lax.axis_size("lon")
    lines = fields * levels
    half = lines // 2
    whole_table = roots_table(2 * columns, columns * lon_count)
    table = whole_table[:columns]
    dma = pltpu.SemaphoreType.DMA
    in_hbm = pl.BlockSpec(memory_space=pl.ANY)
    in_vmem = pl.BlockSpec(memory_space=pltpu.VMEM)
    f32, bf16, i16 = jnp.float32, jnp.bfloat16, jnp.int16
    stepped = pl.pallas_call(
        caps_kernel,
        in_specs=[in_hbm] * 6,
        out_specs=in_vmem,
        out_shape=jax.ShapeDtypeStruct((rows, fields, levels, columns), f32),
        scratch_shapes=[
            pltpu.VMEM((rows + 2, fields, levels, columns), f32),
            pltpu.VMEM((rows, 4, levels, columns), f32),
            pltpu.VMEM((columns, 2 * KC), bf16),
            pltpu.VMEM((2 * KC, columns), bf16),
            pltpu.SMEM(filter_mask.shape, jnp.int32),
            pltpu.SMEM(cutoff_wave.shape, jnp.int32),
            pltpu.VMEM((lines, columns), bf16),
            pltpu.VMEM((lines, columns), bf16),
            pltpu.VMEM((2, fields, levels, columns), bf16),
            pltpu.VMEM((2, fields, levels, columns), bf16),
            pltpu.VMEM((2, rows, 8, 128), f32),
            pltpu.VMEM((2, rows, 8, 128), f32),
            pltpu.VMEM((rows + 1, lines, 2 * KC), f32),
            pltpu.VMEM((rows, half, 2 * KC), f32),
            pltpu.VMEM((rows, half, 2 * KC), i16),
            pltpu.VMEM((rows, half, 2 * KC), i16),
            pltpu.VMEM((RELAYED, half, 2 * KC), i16),
            pltpu.VMEM((rows, lines, 2 * KC), bf16),
            dma((rows,)),
            dma((rows,)),
            dma((4,)),
            dma((2,)),
            dma((2, fields)),
            dma((2,)),
            dma((2, rows)),
            dma((rows,)),
            dma((rows,)),
            dma((rows,)),
            dma((rows,)),
            dma((RELAYED, 2)),
            dma((RELAYED, 2)),
            dma((RELAYED, 2)),
            dma((RELAYED, 2)),
            dma((rows,)),
            dma((rows,)),
        ],
        compiler_params=pltpu.CompilerParams(
            collective_id=1, has_side_effects=True, vmem_limit_bytes=40_000_000
        ),
        name="caps",
    )(
        *(
            pltpu.with_memory_space_constraint(array, pltpu.HBM)
            for array in (
                state_fields,
                stencil_weights,
                filter_mask,
                cutoff_wave,
                jnp.asarray(whole_table.reshape(2, columns, 2 * KC)),
                jnp.asarray(np.ascontiguousarray(table.T)),
            )
        )
    )
    return pl.pallas_call(
        place_kernel,
        in_specs=[in_vmem],
        out_specs=in_hbm,
        out_shape=jax.ShapeDtypeStruct(state_fields.shape, f32),
        scratch_shapes=[dma((rows,))],
        compiler_params=pltpu.CompilerParams(vmem_limit_bytes=1 << 20),
        name="place",
    )(stepped)


def cap_rows(lat_rows):
    return {64: 8, 256: 40}.get(lat_rows, lat_rows)


def solution(mesh):
    def body(state_fields, stencil_weights, filter_mask, cutoff_wave):
        fields, levels, rows, columns = state_fields.shape
        one_block = cap_rows(filter_mask.shape[0]) <= rows
        suits = rows == 8 and columns % 128 == 0 and fields * levels % 32 == 0 and levels % 16 == 0
        if one_block and suits and mesh.shape["lon"] == 4 and mesh.shape["lat"] >= 6:
            return with_caps(state_fields, stencil_weights, filter_mask, cutoff_wave)
        return on_device(state_fields, stencil_weights, filter_mask, cutoff_wave)

    return jax.shard_map(
        body,
        mesh=mesh,
        in_specs=(P(None, None, "lat", "lon"), P(None, None, "lat", "lon"), P(), P()),
        out_specs=P(None, None, "lat", "lon"),
        check_vma=False,
    )
```

```python
import math

import jax
import jax.numpy as jnp
import numpy as np
from jax import lax
from jax.experimental import pallas as pl
from jax.experimental.pallas import tpu as pltpu
from jax.sharding import PartitionSpec as P

KC = 256


def angle_parts(columns, circle_size, axis):
    waves = lax.broadcasted_iota(
        jnp.int32, (columns.size, KC) if axis == 1 else (KC, columns.size), axis
    )
    product = jnp.expand_dims(columns, axis) * waves % circle_size
    angles = product.astype(jnp.float32) * (2.0 * math.pi / circle_size)
    return jnp.cos(angles), jnp.sin(angles)


MESH = pl.DeviceIdType.MESH


def step_kernel(
    state,
    weights,
    cosines,
    sines,
    turned_cosines,
    turned_sines,
    bounds,
    results,
    waves,
    turned,
    rounded,
    top,
    bottom,
    north,
    south,
    columns_out,
    columns_in,
    sides,
    partial,
    halves,
    quarters,
    half_in,
    quarter_in,
    spectra,
    row_send,
    row_recv,
    side_send,
    side_recv,
    sum_send,
    sum_recv,
    join_send,
    join_recv,
):
    fields, lines, columns = state.shape
    chunks, _, size, _ = top.shape
    depth = lines // chunks
    rows = depth // size
    modes = waves.shape[1] // 2
    half = partial.shape[1] // 2
    quarter = half // 2
    lat_count, lon_count = lax.axis_size("lat"), lax.axis_size("lon")
    lat, lon = lax.axis_index("lat"), lax.axis_index("lon")
    after = lax.rem(lon + 1, lon_count)
    before = lax.rem(lon + lon_count - 1, lon_count)
    across = lax.rem(lon + lon_count // 2, lon_count)
    bits = lon_count.bit_length() - 1
    digit = [lax.rem(lon // (1 << b), 2) for b in range(bits)]
    peer = [lon + (1 << b) - (2 << b) * digit[b] for b in range(bits)]
    own_half = digit[0] * half
    own_quarter = digit[1] * quarter

    def span_of(g, first, count):
        return pl.ds(pl.multiple_of(g * depth + first, count), count)

    def remote(source, target, sent, got, device):
        return pltpu.make_async_remote_copy(
            src_ref=source,
            dst_ref=target,
            send_sem=sent,
            recv_sem=got,
            device_id=device,
            device_id_type=MESH,
        )

    def row_copy(g, up, device, into_north):
        return remote(
            top.at[g] if up else bottom.at[g],
            north.at[g] if into_north else south.at[g],
            row_send.at[0 if up else 1, g],
            row_recv.at[0 if into_north else 1, g],
            device,
        )

    def side_copy(k, device):
        return remote(
            columns_out.at[k], columns_in.at[k], side_send.at[k], side_recv.at[k], device
        )

    def sum_copy(b, g):
        if b == 0:
            away = pl.ds(pl.multiple_of((1 - digit[0]) * half, 16), half)
            source, target = partial.at[g, away], half_in.at[g]
        elif b == 1:
            away = pl.ds(pl.multiple_of((1 - digit[1]) * quarter, 16), quarter)
            source, target = halves.at[g, away], quarter_in.at[0, g]
        else:
            source, target = quarters.at[b - 2, g], quarter_in.at[b - 1, g]
        return remote(source, target, sum_send.at[b, g], sum_recv.at[b, g], (lat, peer[b]))

    def join_copy(b, g):
        if b == 0:
            part = pl.ds(pl.multiple_of(own_half, 16), half)
        else:
            part = pl.ds(pl.multiple_of(own_half + own_quarter, 16), quarter)
        view = spectra.at[g, part]
        return remote(view, view, join_send.at[b, g], join_recv.at[b, g], (lat, peer[b]))

    barrier = pltpu.get_barrier_semaphore()
    for other in (after, before, across, *peer):
        pl.semaphore_signal(barrier, inc=1, device_id=(lat, other), device_id_type=MESH)

    @pl.when(lat > 0)
    def _():
        pl.semaphore_signal(barrier, inc=1, device_id=(lat - 1, lon), device_id_type=MESH)

    @pl.when(lat < lat_count - 1)
    def _():
        pl.semaphore_signal(barrier, inc=1, device_id=(lat + 1, lon), device_id_type=MESH)

    inside = (lat > 0) & (lat < lat_count - 1)

    @pl.when(inside)
    def _():
        pl.semaphore_wait(barrier, 5 + bits)

    @pl.when(jnp.logical_not(inside))
    def _():
        pl.semaphore_wait(barrier, 4 + bits)

    taker = lax.broadcasted_iota(jnp.int32, (2 * size, depth), 0)
    taken = lax.broadcasted_iota(jnp.int32, (2 * size, depth), 1)
    wanted = jnp.where(taker < size, taker * rows, (taker - size) * rows + rows - 1)
    gather = jnp.where(taken == wanted, 1.0, 0.0).astype(jnp.bfloat16)

    def send_rows(g, carry):
        for field in range(fields):
            sign = -1.0 if field < 2 else 1.0
            up_sign = jnp.where(lat == 0, sign, 1.0).astype(jnp.float32)
            down_sign = jnp.where(lat == lat_count - 1, sign, 1.0).astype(jnp.float32)
            edges = jnp.dot(
                gather,
                state[field, span_of(g, 0, depth)].astype(jnp.bfloat16),
                preferred_element_type=jnp.float32,
            )
            top[g, field] = (edges[:size] * up_sign).astype(jnp.bfloat16)
            bottom[g, field] = (edges[size:] * down_sign).astype(jnp.bfloat16)

        @pl.when(lat == 0)
        def _():
            row_copy(g, True, (lat, across), True).start()

        @pl.when(lat > 0)
        def _():
            row_copy(g, True, (lat - 1, lon), False).start()

        @pl.when(lat < lat_count - 1)
        def _():
            row_copy(g, False, (lat + 1, lon), True).start()

        @pl.when(lat == lat_count - 1)
        def _():
            row_copy(g, False, (lat, across), False).start()

        return carry

    lax.fori_loop(0, chunks, send_rows, 0)

    spot = lax.broadcasted_iota(jnp.int32, (16, 128), 1)
    line = lax.broadcasted_iota(jnp.int32, (16, 128), 0)

    def pick(k, lanes, lane):
        chosen = jnp.where((spot == lane) & (line == 0), 1.0, 0.0).astype(jnp.bfloat16)
        for g in range(chunks):
            for field in range(0, fields):
                first = (g * fields + field) * depth
                edge = state[field, span_of(g, 0, depth), lanes].astype(jnp.bfloat16)
                picked = lax.dot_general(
                    chosen, edge, (((1,), (1,)), ((), ())), preferred_element_type=jnp.float32
                )
                columns_out[k, g * fields + field] = picked.astype(jnp.bfloat16)

    pick(0, pl.ds(columns - 128, 128), 127)
    side_copy(0, (lat, after)).start()
    pick(1, pl.ds(0, 128), 0)
    side_copy(1, (lat, before)).start()

    fine = 32
    coarse = columns // fine
    fine_cos, fine_sin = cosines[coarse:], sines[coarse:]

    def fill(at, carry):
        span = pl.ds(pl.multiple_of(at * fine, fine), fine)
        coarse_cos, coarse_sin = cosines[pl.ds(at, 1)], sines[pl.ds(at, 1)]
        waves[span, :modes] = (coarse_cos * fine_cos - coarse_sin * fine_sin).astype(jnp.bfloat16)
        waves[span, modes:] = (coarse_sin * fine_cos + coarse_cos * fine_sin).astype(jnp.bfloat16)
        return carry

    lax.fori_loop(0, coarse, fill, 0)
    lane_cos, lane_sin = turned_cosines[:, :128], turned_sines[:, :128]
    for at in range(columns // 128):
        span = pl.ds(at * 128, 128)
        tile_cos = turned_cosines[:, 128 + at : 129 + at]
        tile_sin = turned_sines[:, 128 + at : 129 + at]
        turned[:modes, span] = (tile_cos * lane_cos - tile_sin * lane_sin).astype(jnp.bfloat16)
        turned[modes:, span] = (tile_sin * lane_cos + tile_cos * lane_sin).astype(jnp.bfloat16)

    spread = jnp.where(line == 0, 1.0, 0.0).astype(jnp.bfloat16)
    for k in range(2):
        side_copy(k, (lat, after)).wait_recv()
        for at in range(chunks * fields):
            sides[k, at] = lax.dot_general(
                columns_in[k, at],
                spread,
                (((0,), (0,)), ((), ())),
                preferred_element_type=jnp.float32,
            )

    lane = lax.broadcasted_iota(jnp.int32, (rows, columns), 1)
    level_line = lax.broadcasted_iota(jnp.int32, (rows, columns), 0)
    copies = columns // 128

    wave = lax.rem(lax.broadcasted_iota(jnp.int32, (rows, 2 * modes), 1), modes)
    circle_size = columns * lon_count
    weight = jnp.where(wave == 0, 1.0 / circle_size, 2.0 / circle_size)
    scale = jnp.where(wave <= bounds[:, 1:2], weight, 0.0).astype(jnp.float32)

    def advance(g):
        row_copy(g, True, (lat, across), True).wait_recv()
        row_copy(g, False, (lat, across), False).wait_recv()

        def one_field(field, inner):
            above = north[g, field].astype(jnp.float32)
            below = south[g, field].astype(jnp.float32)
            for level in range(0, size, 2):
                pair = []
                for at in (level, level + 1):
                    span = pl.ds(at * rows, rows)
                    here = span_of(g, at * rows, rows)
                    x = state[field, here]
                    left = jnp.concatenate([sides[0, g * fields + field, span]] * copies, axis=1)
                    right = jnp.concatenate([sides[1, g * fields + field, span]] * copies, axis=1)
                    w = jnp.where(lane == 0, left, pltpu.roll(x, 1, 1))
                    e = jnp.where(lane == columns - 1, right, pltpu.roll(x, columns - 1, 1))
                    n = jnp.where(level_line == 0, above[at : at + 1], pltpu.roll(x, 1, 0))
                    s = jnp.where(
                        level_line == rows - 1, below[at : at + 1], pltpu.roll(x, rows - 1, 0)
                    )
                    y = (
                        x
                        + weights[0, here] * (e - x)
                        + weights[1, here] * (w - x)
                        + weights[2, here] * (n - x)
                        + weights[3, here] * (s - x)
                    )
                    results[field, here] = y
                    pair.append(y)
                first = pl.multiple_of(field * depth + level * rows, 2 * rows)
                rounded[pl.ds(first, 2 * rows), :] = jnp.concatenate(pair, axis=0).astype(
                    jnp.bfloat16
                )
            return inner

        lax.fori_loop(0, fields, one_field, 0)
        partial[g] = jnp.dot(rounded[...], waves[...], preferred_element_type=jnp.float32)
        sum_copy(0, g).start()

    def pair_sum(g):
        sum_copy(0, g).wait_recv()
        mine = pl.ds(pl.multiple_of(own_half, 16), half)
        halves[g] = partial[g, mine] + half_in[g]
        sum_copy(1, g).start()

    def full_sum(g):
        sum_copy(1, g).wait_recv()
        mine = pl.ds(pl.multiple_of(own_quarter, 16), quarter)
        total = halves[g, mine] + quarter_in[0, g]
        for b in range(2, bits):
            quarters[b - 2, g] = total
            sum_copy(b, g).start()
            sum_copy(b, g).wait_recv()
            total = total + quarter_in[b - 1, g]
        scaled = total.reshape(quarter // rows, rows, 2 * modes) * scale[None]
        part = pl.ds(pl.multiple_of(own_half + own_quarter, 16), quarter)
        spectra[g, part] = scaled.reshape(quarter, 2 * modes).astype(jnp.bfloat16)
        join_copy(1, g).start()

    def join(g):
        join_copy(1, g).wait_recv()
        join_copy(0, g).start()

    def merge(g):
        join_copy(0, g).wait_recv()
        smooth = jnp.dot(spectra[g], turned[...], preferred_element_type=jnp.float32)
        smooth = smooth.astype(jnp.bfloat16).astype(jnp.float32)
        smooth = smooth.reshape(fields, size, rows, columns)
        kept = jnp.broadcast_to(bounds[:, 0:1], (rows, columns)) != 0
        for field in range(fields):
            for at in range(size):
                here = span_of(g, at * rows, rows)
                results[field, here] = jnp.where(kept, smooth[field, at], results[field, here])

    def forward(t, carry):
        advance(t)

        @pl.when(t >= 1)
        def _():
            pair_sum(t - 1)

        return carry

    last = chunks - 1
    lax.fori_loop(0, chunks, forward, 0)
    full_sum(0)
    pair_sum(last)

    def sums(g, carry):
        full_sum(g)
        return carry

    def joins(g, carry):
        join(g)
        return carry

    def merges(g, carry):
        merge(g)

        @pl.when(g + 2 < chunks)
        def _():
            join(g + 2)

        return carry

    lax.fori_loop(1, last, sums, 0)
    lax.fori_loop(0, 2, joins, 0)
    full_sum(last)
    lax.fori_loop(0, chunks, merges, 0)

    def finish(g, carry):
        for b in range(bits):
            sum_copy(b, g).wait_send()
        for b in range(2):
            join_copy(b, g).wait_send()
        row_copy(g, True, (lat, across), True).wait_send()
        row_copy(g, False, (lat, across), False).wait_send()
        return carry

    lax.fori_loop(0, chunks, finish, 0)
    for k in range(2):
        side_copy(k, (lat, after)).wait_send()


def on_device(state_fields, stencil_weights, filter_mask, cutoff_wave):
    fields, levels, rows, columns = state_fields.shape
    lat_count, lon_count = lax.axis_size("lat"), lax.axis_size("lon")
    lat_pos, lon_pos = lax.axis_index("lat"), lax.axis_index("lon")
    circle_size = columns * lon_count
    size = 8
    steps = levels // size
    start = lat_pos * rows
    bounds = lax.dynamic_slice_in_dim(jnp.stack([filter_mask, cutoff_wave], axis=1), start, rows)
    origin = lon_pos * columns
    cosines, sines = angle_parts(
        jnp.concatenate(
            [origin + 32 * jnp.arange(columns // 32), jnp.arange(32)]
        ).astype(jnp.int32),
        circle_size,
        1,
    )
    turned_cosines, turned_sines = angle_parts(
        jnp.concatenate(
            [jnp.arange(128), origin + 128 * jnp.arange(columns // 128)]
        ).astype(jnp.int32),
        circle_size,
        0,
    )
    rows_each = fields * size * rows
    depth = size * rows
    dma = pltpu.SemaphoreType.DMA
    strip = pltpu.VMEM((steps, fields, size, columns), jnp.bfloat16)
    column_strip = pltpu.VMEM((2, steps * fields, 16, depth), jnp.bfloat16)
    extra = max(lon_count.bit_length() - 3, 1)
    in_vmem = pl.BlockSpec(memory_space=pltpu.VMEM)
    bits = lon_count.bit_length() - 1
    advanced = pl.pallas_call(
        step_kernel,
        in_specs=[in_vmem] * 7,
        out_specs=in_vmem,
        out_shape=jax.ShapeDtypeStruct((fields, levels * rows, columns), jnp.float32),
        scratch_shapes=[
            pltpu.VMEM((columns, 2 * KC), jnp.bfloat16),
            pltpu.VMEM((2 * KC, columns), jnp.bfloat16),
            pltpu.VMEM((rows_each, columns), jnp.bfloat16),
            strip,
            strip,
            strip,
            strip,
            column_strip,
            column_strip,
            pltpu.VMEM((2, steps * fields, depth, 128), jnp.float32),
            pltpu.VMEM((steps, rows_each, 2 * KC), jnp.float32),
            pltpu.VMEM((steps, rows_each // 2, 2 * KC), jnp.float32),
            pltpu.VMEM((extra, steps, rows_each // 4, 2 * KC), jnp.float32),
            pltpu.VMEM((steps, rows_each // 2, 2 * KC), jnp.float32),
            pltpu.VMEM((bits - 1, steps, rows_each // 4, 2 * KC), jnp.float32),
            pltpu.VMEM((steps, rows_each, 2 * KC), jnp.bfloat16),
            dma((2, steps)),
            dma((2, steps)),
            dma((2,)),
            dma((2,)),
            dma((bits, steps)),
            dma((bits, steps)),
            dma((2, steps)),
            dma((2, steps)),
        ],
        compiler_params=pltpu.CompilerParams(
            collective_id=0, has_side_effects=True, vmem_limit_bytes=38 << 20
        ),
        name="step",
    )(
        state_fields.reshape(fields, levels * rows, columns),
        stencil_weights.reshape(4, levels * rows, columns),
        cosines,
        sines,
        turned_cosines,
        turned_sines,
        bounds,
    )
    return advanced.reshape(state_fields.shape)


def roots_table(columns, circle_size):
    steps = np.arange(columns)[:, None] * np.arange(KC)[None, :] % circle_size
    angles = steps * (2.0 * np.pi / circle_size)
    return np.concatenate([np.cos(angles), np.sin(angles)], axis=1).astype(jnp.bfloat16)


def quarter_turns(shape, axis, turns):
    phase = lax.rem(lax.broadcasted_iota(jnp.int32, shape, axis) * turns, 4)
    a = jnp.where(phase == 0, 1.0, jnp.where(phase == 2, -1.0, 0.0))
    b = jnp.where(phase == 1, 1.0, jnp.where(phase == 3, -1.0, 0.0))
    return a.astype(jnp.bfloat16), b.astype(jnp.bfloat16)


RELAYED = 2


def caps_kernel(
    state,
    weights,
    mask_in,
    cutoff_in,
    waves_in,
    turned_in,
    results,
    xs,
    ws,
    waves,
    turned,
    mask,
    cutoff,
    even_lines,
    odd_lines,
    edges,
    halos,
    columns_out,
    columns_in,
    partial,
    half_in,
    coded,
    coded_in,
    passing,
    spectra,
    state_sem,
    weight_sem,
    table_sem,
    edge_send,
    edge_recv,
    column_send,
    column_recv,
    half_send,
    half_recv,
    code_send,
    code_recv,
    lend_send,
    lend_recv,
    pass_send,
    pass_recv,
    join_send,
    join_recv,
):
    rows, fields, levels, columns = results.shape
    groups = levels // 8
    lines = fields * levels
    half = lines // 2
    lat_count, lon_count = lax.axis_size("lat"), lax.axis_size("lon")
    lat, lon = lax.axis_index("lat"), lax.axis_index("lon")
    after = lax.rem(lon + 1, lon_count)
    before = lax.rem(lon + lon_count - 1, lon_count)
    across = lax.rem(lon + lon_count // 2, lon_count)
    core = lax.rem(lon, 2)
    partner = lon + 1 - 2 * core
    circle_size = columns * lon_count
    first, last = lat == 0, lat == lat_count - 1
    polar = first | last
    middle = (lat == 2) | (lat == lat_count - 3)
    helper = jnp.where(first, 2, lat_count - 3)
    served = jnp.where(lat == 2, 0, lat_count - 1)
    edge_row = jnp.where(last, 0, rows - 1)

    def row_at(i):
        return jnp.where(i < rows - 2, i + 1, jnp.where(i == rows - 2, edge_row, rows - 1 - edge_row))

    own = pl.ds(pl.multiple_of(core * half, 16), half)
    other = pl.ds(pl.multiple_of((1 - core) * half, 16), half)

    def remote(source, target, sent, got, device):
        return pltpu.make_async_remote_copy(
            src_ref=source,
            dst_ref=target,
            send_sem=sent,
            recv_sem=got,
            device_id=device,
            device_id_type=MESH,
        )

    def state_copy(r):
        return pltpu.make_async_copy(state.at[:, :, r], xs.at[r + 1], state_sem.at[r])

    def weight_copy(r):
        return pltpu.make_async_copy(weights.at[:, :, r], ws.at[r], weight_sem.at[r])

    def table_copies():
        return (
            pltpu.make_async_copy(waves_in.at[core], waves, table_sem.at[0]),
            pltpu.make_async_copy(turned_in, turned, table_sem.at[1]),
        )

    def bound_copies():
        return (
            pltpu.make_async_copy(mask_in, mask, table_sem.at[2]),
            pltpu.make_async_copy(cutoff_in, cutoff, table_sem.at[3]),
        )

    def edge_copy(k, field, side, device):
        return remote(
            edges.at[k, field],
            halos.at[side, field],
            edge_send.at[k],
            edge_recv.at[side, field],
            device,
        )

    def column_copy(k, r, device):
        return remote(
            columns_out.at[k, r],
            columns_in.at[k, r],
            column_send.at[k],
            column_recv.at[k, r],
            device,
        )

    def half_copy(i):
        return remote(
            partial.at[i, other], half_in.at[i], half_send.at[i], half_recv.at[i], (lat, partner)
        )

    def code_copy(i):
        return remote(
            coded.at[i], coded_in.at[i], code_send.at[i], code_recv.at[i], (lat, across)
        )

    first_piece = (half // 2 + 15) // 16 * 16
    pieces = (pl.ds(0, first_piece), pl.ds(first_piece, half - first_piece))

    def lend_copy(i, k):
        return remote(
            coded.at[i, pieces[k]],
            passing.at[i, pieces[k]],
            lend_send.at[i, k],
            pass_recv.at[i, k],
            (helper, across),
        )

    def pass_copy(i, k):
        return remote(
            passing.at[i, pieces[k]],
            coded_in.at[i, pieces[k]],
            pass_send.at[i, k],
            lend_recv.at[i, k],
            (served, lon),
        )

    def join_copy(i):
        view = spectra.at[i, own]
        return remote(view, view, join_send.at[i], join_recv.at[i], (lat, partner))

    barrier = pltpu.get_barrier_semaphore()

    def greet(a, b):
        pl.semaphore_signal(barrier, inc=1, device_id=(a, b), device_id_type=MESH)

    for b in (after, before, across):
        greet(lat, b)

    @pl.when(lat > 0)
    def _():
        greet(lat - 1, lon)

    @pl.when(lat < lat_count - 1)
    def _():
        greet(lat + 1, lon)

    @pl.when(polar)
    def _():
        greet(helper, lon)
        greet(helper, across)

    @pl.when(middle)
    def _():
        greet(served, lon)
        greet(served, across)

    for r in (0, rows - 1, *range(1, rows - 1)):
        state_copy(r).start()

    @pl.when(polar)
    def _():
        for copy in table_copies():
            copy.start()

    for copy in bound_copies():
        copy.start()
    for r in (*range(1, rows - 1), 0, rows - 1):
        weight_copy(r).start()

    for r in (0, rows - 1):
        state_copy(r).wait()
    for field in range(fields):
        sign = -1.0 if field < 2 else 1.0
        up_sign = jnp.where(first, sign, 1.0).astype(jnp.float32)
        down_sign = jnp.where(last, sign, 1.0).astype(jnp.float32)
        edges[0, field] = (xs[1, field] * up_sign).astype(jnp.bfloat16)
        edges[1, field] = (xs[rows, field] * down_sign).astype(jnp.bfloat16)

    @pl.when(polar)
    def _():
        pl.semaphore_wait(barrier, 3 + 1 + 2)

    @pl.when(middle)
    def _():
        pl.semaphore_wait(barrier, 3 + 2 + 2)

    @pl.when(jnp.logical_not(polar | middle))
    def _():
        pl.semaphore_wait(barrier, 3 + 2)

    def send_up(field):
        @pl.when(lat > 0)
        def _():
            edge_copy(0, field, 1, (lat - 1, lon)).start()

    def send_down(field):
        @pl.when(lat < lat_count - 1)
        def _():
            edge_copy(1, field, 0, (lat + 1, lon)).start()

    beside_first, beside_last = lat == 1, lat == lat_count - 2

    @pl.when(beside_first)
    def _():
        for field in range(fields):
            send_up(field)
        for field in range(fields):
            send_down(field)

    @pl.when(beside_last)
    def _():
        for field in range(fields):
            send_down(field)
        for field in range(fields):
            send_up(field)

    @pl.when(jnp.logical_not(beside_first | beside_last))
    def _():
        for field in range(fields):
            send_up(field)
            send_down(field)

    spot = lax.broadcasted_iota(jnp.int32, (8, 128), 1)

    def send_columns(r):
        to_after = jnp.zeros((8, 128), jnp.float32)
        to_before = jnp.zeros((8, 128), jnp.float32)
        for group in range(groups):
            for field in range(fields):
                at = group * fields + field
                span = pl.ds(group * 8, 8)
                right = xs[r + 1, field, span, pl.ds(columns - 128, 128)]
                left = xs[r + 1, field, span, pl.ds(0, 128)]
                to_after = jnp.where(spot == at, pltpu.roll(right, at + 1, 1), to_after)
                left = pltpu.roll(left, at, 1) if at else left
                to_before = jnp.where(spot == at, left, to_before)
        columns_out[0, r] = to_after
        columns_out[1, r] = to_before
        column_copy(0, r, (lat, after)).start()
        column_copy(1, r, (lat, before)).start()

    def send_rim(field):
        @pl.when(first)
        def _():
            edge_copy(0, field, 0, (lat, across)).start()

        @pl.when(last)
        def _():
            edge_copy(1, field, 1, (lat, across)).start()

    for r in (*range(1, rows - 1), rows - 1, 0):
        if 0 < r < rows - 1:
            state_copy(r).wait()
        send_columns(r)
        if r == 3:
            send_rim(0)
    for field in range(1, fields):
        send_rim(field)

    for copy in bound_copies():
        copy.wait()

    def turn_back():
        table_copies()[1].wait()
        a, b = quarter_turns((16, 128), 0, core)

        def turn(t, carry):
            low = pl.ds(pl.multiple_of(t * 16, 16), 16)
            high = pl.ds(pl.multiple_of(KC + t * 16, 16), 16)
            for tile in range(columns // 128):
                lanes = pl.ds(tile * 128, 128)
                c, s = turned[low, lanes], turned[high, lanes]
                turned[low, lanes] = a * c - b * s
                turned[high, lanes] = a * s + b * c
            return carry

        lax.fori_loop(0, KC // 16, turn, 0)

    tiles = columns // 128

    def shares(r, group):
        span = pl.ds(group * 8, 8)
        return [ws[r, q, span] for q in range(4)]

    def advanced(r, field, group, east_w, west_w, north_w, south_w):
        at = group * fields + field
        span = pl.ds(group * 8, 8)
        x = xs[r + 1, field, span]
        n = xs[r, field, span]
        s = xs[r + 2, field, span]
        parts = [x[:, t * 128 : t * 128 + 128] for t in range(tiles)]
        left = columns_in[0, r]
        left = pltpu.roll(left, 128 - at, 1) if at else left
        right = pltpu.roll(columns_in[1, r], 127 - at, 1)
        to_right = [left] + [pltpu.roll(p, 1, 1) for p in parts]
        to_left = [pltpu.roll(p, 127, 1) for p in parts] + [right]
        w = [jnp.where(spot == 0, to_right[t], to_right[t + 1]) for t in range(tiles)]
        e = [jnp.where(spot == 127, to_left[t + 1], to_left[t]) for t in range(tiles)]
        y = (
            x
            + east_w * (jnp.concatenate(e, axis=1) - x)
            + west_w * (jnp.concatenate(w, axis=1) - x)
            + north_w * (n - x)
            + south_w * (s - x)
        )
        results[r, field, span] = y
        return y

    def ready(r):
        column_copy(0, r, (lat, after)).wait_recv()
        column_copy(1, r, (lat, before)).wait_recv()
        weight_copy(r).wait()

    def step(r):
        for group in range(groups):
            weight = shares(r, group)
            for field in range(fields):
                advanced(r, field, group, *weight)

    def step_into(r, target):
        for group in range(0, groups, 2):
            weight, next_weight = shares(r, group), shares(r, group + 1)
            for field in range(fields):
                pair = (
                    advanced(r, field, group, *weight),
                    advanced(r, field, group + 1, *next_weight),
                )
                target[pl.ds(field * levels + group * 8, 16)] = jnp.concatenate(
                    pair, axis=0
                ).astype(jnp.bfloat16)

    def transform(source, i):
        partial[i] = jnp.dot(source[...], waves[...], preferred_element_type=jnp.float32)

    def combine(i):
        half_copy(i).wait_recv()
        total = partial[i, own] + half_in[i]
        partial[i, own] = total
        largest = jnp.maximum(jnp.max(jnp.abs(total), axis=1, keepdims=True), 1e-30)
        power = jnp.ceil(jnp.log2(largest))
        code = jnp.round(total * (jnp.exp2(-power) * 32767.0))
        code = jnp.clip(code, -32767.0, 32767.0)
        place = lax.broadcasted_iota(jnp.int32, (half, 2 * KC), 1)
        code = jnp.where(place == KC, power, code)
        coded[i] = code.astype(jnp.int32).astype(jnp.int16)

    wave = lax.rem(lax.broadcasted_iota(jnp.int32, (8, 2 * KC), 1), KC)
    weight = jnp.where(wave == 0, 1.0 / circle_size, 2.0 / circle_size).astype(jnp.float32)

    def finish(i):
        @pl.when(i < RELAYED)
        def _():
            for k in range(2):
                pass_copy(i, k).wait_recv()

        @pl.when(i >= RELAYED)
        def _():
            code_copy(i).wait_recv()

        code = coded_in[i].astype(jnp.int32).astype(jnp.float32)
        unit = jnp.exp2(code[:, KC : KC + 1]) * (1.0 / 32767.0)
        place = lax.broadcasted_iota(jnp.int32, (half, 2 * KC), 1)
        turned_by = jnp.where(lax.rem(place, 2) == 0, 1.0, -1.0)
        code = code * jnp.where(place == KC, 0.0, turned_by)
        total = partial[i, own] + code * unit
        limit = cutoff[lat * rows + row_at(i)]
        scale = jnp.where(wave <= limit, weight, 0.0)
        scaled = total.reshape(half // 8, 8, 2 * KC) * scale[None]
        spectra[i, own] = scaled.reshape(half, 2 * KC).astype(jnp.bfloat16)
        join_copy(i).start()

    def merge(i):
        join_copy(i).wait_recv()
        r = row_at(i)
        smooth = jnp.dot(spectra[i], turned[...], preferred_element_type=jnp.float32)
        smooth = smooth.astype(jnp.bfloat16).astype(jnp.float32)
        smooth = smooth.reshape(fields, levels, columns)
        kept = jnp.full((8, columns), mask[lat * rows + r], jnp.int32) != 0
        for field in range(fields):
            for group in range(groups):
                span = pl.ds(group * 8, 8)
                results[r, field, span] = jnp.where(
                    kept, smooth[field, group * 8 : group * 8 + 8], results[r, field, span]
                )

    def send_code(i):
        @pl.when(i < RELAYED)
        def _():
            for k in range(2):
                lend_copy(i, k).start()

        @pl.when(i >= RELAYED)
        def _():
            code_copy(i).start()

    def combine_and_send(i):
        combine(i)
        send_code(i)

    pairs = (rows - 2) // 2

    @pl.when(polar)
    def _():
        table_copies()[0].wait()
        turn_back()
        odd_lines[...] = jnp.zeros_like(odd_lines)

        def two_rows(j, carry):
            i = 2 * j
            ready(i + 1)
            transform(odd_lines, jnp.where(j == 0, rows, i - 1))
            step_into(i + 1, even_lines)

            @pl.when(j >= 1)
            def _():
                half_copy(i - 1).start()

            @pl.when(j >= 2)
            def _():
                combine_and_send(i - 4)

            ready(i + 2)
            transform(even_lines, i)
            step_into(i + 2, odd_lines)
            half_copy(i).start()

            @pl.when(j >= 2)
            def _():
                combine_and_send(i - 3)

            return carry

        lax.fori_loop(0, pairs, two_rows, 0)
        transform(odd_lines, rows - 3)
        half_copy(rows - 3).start()
        combine_and_send(rows - 6)
        combine_and_send(rows - 5)
        combine_and_send(rows - 4)
        combine_and_send(rows - 3)

    @pl.when(jnp.logical_not(polar))
    def _():
        def one_row(r, carry):
            ready(r)
            step(r)
            return carry

        lax.fori_loop(1, rows - 1, one_row, 0)

    @pl.when(middle)
    def _():
        for p in range(RELAYED):
            for k in range(2):
                lend_copy(p, k).wait_recv()
                pass_copy(p, k).start()

    def edge_step(i, carry):
        r = row_at(i)
        side = jnp.where(r == 0, 0, 1)
        ready(r)
        for field in range(fields):
            edge_copy(0, field, side, (lat, across)).wait_recv()
            xs[side * (rows + 1), field] = halos[side, field].astype(jnp.float32)
            for group in range(groups):
                advanced(r, field, group, *shares(r, group))

        @pl.when(polar)
        def _():
            even_lines[...] = results[r].reshape(lines, columns).astype(jnp.bfloat16)
            transform(even_lines, i)
            half_copy(i).start()

        return carry

    lax.fori_loop(rows - 2, rows, edge_step, 0)

    @pl.when(polar)
    def _():
        def position(t):
            return jnp.where(t < 2 * RELAYED, t // 2 + RELAYED * (1 - lax.rem(t, 2)), t)

        combine_and_send(rows - 2)
        combine_and_send(rows - 1)
        finish(position(0))
        finish(position(1))

        def endings(t, carry):
            merge(position(t - 2))
            finish(position(t))
            return carry

        lax.fori_loop(2, rows - 1, endings, 0)
        merge(position(rows - 3))
        merge(position(rows - 2))
        finish(rows - 1)
        merge(rows - 1)

        def drain(i, carry):
            half_copy(i).wait_send()
            join_copy(i).wait_send()

            @pl.when(i < RELAYED)
            def _():
                for k in range(2):
                    lend_copy(i, k).wait_send()

            @pl.when(i >= RELAYED)
            def _():
                code_copy(i).wait_send()

            return carry

        lax.fori_loop(0, rows, drain, 0)

    @pl.when(middle)
    def _():
        for p in range(RELAYED):
            for k in range(2):
                pass_copy(p, k).wait_send()

    for k in range(2):
        remote(
            edges.at[k], halos.at[k], edge_send.at[k], edge_recv.at[k, 0], (lat, across)
        ).wait_send()
        remote(
            columns_out.at[k],
            columns_in.at[k],
            column_send.at[k],
            column_recv.at[k, 0],
            (lat, after),
        ).wait_send()


def place_kernel(stepped, out, sem):
    copies = [
        pltpu.make_async_copy(stepped.at[r], out.at[:, :, r], sem.at[r])
        for r in range(stepped.shape[0])
    ]
    for copy in copies:
        copy.start()
    for copy in copies:
        copy.wait()


def with_caps(state_fields, stencil_weights, filter_mask, cutoff_wave):
    fields, levels, rows, columns = state_fields.shape
    lon_count = lax.axis_size("lon")
    lines = fields * levels
    half = lines // 2
    whole_table = roots_table(2 * columns, columns * lon_count)
    table = whole_table[:columns]
    dma = pltpu.SemaphoreType.DMA
    in_hbm = pl.BlockSpec(memory_space=pl.ANY)
    in_vmem = pl.BlockSpec(memory_space=pltpu.VMEM)
    f32, bf16, i16 = jnp.float32, jnp.bfloat16, jnp.int16
    stepped = pl.pallas_call(
        caps_kernel,
        in_specs=[in_hbm] * 6,
        out_specs=in_vmem,
        out_shape=jax.ShapeDtypeStruct((rows, fields, levels, columns), f32),
        scratch_shapes=[
            pltpu.VMEM((rows + 2, fields, levels, columns), f32),
            pltpu.VMEM((rows, 4, levels, columns), f32),
            pltpu.VMEM((columns, 2 * KC), bf16),
            pltpu.VMEM((2 * KC, columns), bf16),
            pltpu.SMEM(filter_mask.shape, jnp.int32),
            pltpu.SMEM(cutoff_wave.shape, jnp.int32),
            pltpu.VMEM((lines, columns), bf16),
            pltpu.VMEM((lines, columns), bf16),
            pltpu.VMEM((2, fields, levels, columns), bf16),
            pltpu.VMEM((2, fields, levels, columns), bf16),
            pltpu.VMEM((2, rows, 8, 128), f32),
            pltpu.VMEM((2, rows, 8, 128), f32),
            pltpu.VMEM((rows + 1, lines, 2 * KC), f32),
            pltpu.VMEM((rows, half, 2 * KC), f32),
            pltpu.VMEM((rows, half, 2 * KC), i16),
            pltpu.VMEM((rows, half, 2 * KC), i16),
            pltpu.VMEM((RELAYED, half, 2 * KC), i16),
            pltpu.VMEM((rows, lines, 2 * KC), bf16),
            dma((rows,)),
            dma((rows,)),
            dma((4,)),
            dma((2,)),
            dma((2, fields)),
            dma((2,)),
            dma((2, rows)),
            dma((rows,)),
            dma((rows,)),
            dma((rows,)),
            dma((rows,)),
            dma((RELAYED, 2)),
            dma((RELAYED, 2)),
            dma((RELAYED, 2)),
            dma((RELAYED, 2)),
            dma((rows,)),
            dma((rows,)),
        ],
        compiler_params=pltpu.CompilerParams(
            collective_id=1, has_side_effects=True, vmem_limit_bytes=40_000_000
        ),
        name="caps",
    )(
        *(
            pltpu.with_memory_space_constraint(array, pltpu.HBM)
            for array in (
                state_fields,
                stencil_weights,
                filter_mask,
                cutoff_wave,
                jnp.asarray(whole_table.reshape(2, columns, 2 * KC)),
                jnp.asarray(np.ascontiguousarray(table.T)),
            )
        )
    )
    return pl.pallas_call(
        place_kernel,
        in_specs=[in_vmem],
        out_specs=in_hbm,
        out_shape=jax.ShapeDtypeStruct(state_fields.shape, f32),
        scratch_shapes=[dma((rows,))],
        compiler_params=pltpu.CompilerParams(vmem_limit_bytes=1 << 20),
        name="place",
    )(stepped)


def cap_rows(lat_rows):
    return {64: 8, 256: 40}.get(lat_rows, lat_rows)


def solution(mesh):
    def body(state_fields, stencil_weights, filter_mask, cutoff_wave):
        fields, levels, rows, columns = state_fields.shape
        one_block = cap_rows(filter_mask.shape[0]) <= rows
        suits = rows == 8 and columns % 128 == 0 and fields * levels % 32 == 0 and levels % 16 == 0
        if one_block and suits and mesh.shape["lon"] == 4 and mesh.shape["lat"] >= 6:
            return with_caps(state_fields, stencil_weights, filter_mask, cutoff_wave)
        return on_device(state_fields, stencil_weights, filter_mask, cutoff_wave)

    return jax.shard_map(
        body,
        mesh=mesh,
        in_specs=(P(None, None, "lat", "lon"), P(None, None, "lat", "lon"), P(), P()),
        out_specs=P(None, None, "lat", "lon"),
        check_vma=False,
    )
```
